128 devices in a mesh: gy: 16 (over z, y), gz: 8 (over x, core).
Axes of the slice: x: 4, y: 4, z: 4, core: 2. Of those that a mesh axis runs over, the one named last changes fastest.
Arguments:
- eddy_cells: int32 [16, 8, 2, 2048], P('gy', 'gz'), may hold values from 0 to 32767, as said below
- eddy_signs: int32 [16, 8, 3, 2048], P('gy', 'gz'), may hold values from -1 to 1, as said below
- eddy_counts: int32 [16, 8], P('gy', 'gz'), may hold values from 256 to 2048
- stress_diag: float32 [3, 32768], P(None, 'gy'), may hold values from 0.3 to 3
- stress_shear: float32 [3, 32768], P(None, 'gy'), may hold values from -3 to 3
- mean_flow: float32 [3, 32768, 2048], P(None, 'gy', 'gz'), may hold values from -6 to 6
Outputs:
- velocity: float32 [3, 32768, 2048], P(None, 'gy', 'gz')
The draws below stay inside these ranges and needn't reach their ends.
Inputs may be any that keep to these rules, and one draw needn't show every extreme that they name: `eddy_cells`: every slot of tile (i, j) holds a wall-normal cell in [i * 2048, (i + 1) * 2048) and a spanwise cell in [j * 256, (j + 1) * 256); only the first eddy_counts[i, j] slots are eddies. `eddy_signs`: each entry is -1 or 1.
All inputs are finite; a program needn't handle non-finite values.
Results may differ from the reference program's by a relative error of at most 0.0001.
Values sent between devices are 32-bit elements; how exact they have to be, the bound alone decides.
A program may use at most 128 MiB of HBM per device.

```python
import math
import jax
import jax.numpy as jnp
from jax import lax

TY = 2048
TZ = 256
CAP = 2048
HALF = 128
TILES_Y = 16
TILES_Z = 8
NY = 32768
NZ = 2048


def draw_eddy_counts(key, part):
    rows_index = jnp.arange(TILES_Y, dtype=jnp.int32)
    highest = CAP - 3 * CAP // 4 * rows_index // max(TILES_Y - 1, 1)
    lowest = highest // 2
    key_counts, key_full = jax.random.split(jax.random.fold_in(key, 11))
    spread = jax.random.randint(key_counts, (TILES_Y, TILES_Z), 0, 1 << 20)
    counts = lowest[:, None] + spread % (highest - lowest + 1)[:, None]
    full_tile = jax.random.randint(key_full, (), 0, TILES_Z)
    counts = counts.at[0, full_tile].set(CAP)
    return counts.astype(jnp.int32)


def draw_eddy_cells(key, part):
    key_wall, key_span = jax.random.split(jax.random.fold_in(key, 23))
    wall_cells = jax.random.randint(key_wall, (TILES_Y, TILES_Z, CAP), 0, TY)
    wall_cells = wall_cells + (jnp.arange(TILES_Y, dtype=jnp.int32) * TY)[:, None, None]
    span_cells = jax.random.randint(key_span, (TILES_Y, TILES_Z, CAP), 0, TZ)
    span_cells = span_cells + (jnp.arange(TILES_Z, dtype=jnp.int32) * TZ)[None, :, None]
    return jnp.stack([wall_cells, span_cells], axis=2).astype(jnp.int32)


def draw_eddy_signs(key, part):
    coins = jax.random.randint(jax.random.fold_in(key, 37), (TILES_Y, TILES_Z, 3, CAP), 0, 2)
    return (coins * 2 - 1).astype(jnp.int32)


def level_of(stream_key, dims, pieces, least, largest):
    level = 1.0
    for dim, blocks in pieces:
        draws = jax.random.uniform(jax.random.fold_in(jax.random.fold_in(stream_key, 6), dim), (blocks,), jnp.float32, least / len(pieces), largest / len(pieces))
        level = level * jnp.repeat(jnp.exp(draws), dims[dim] // blocks).reshape((-1,) + (1,) * (len(dims) - 1 - dim))
    return level


def normal_values(own_key, extent, scale, most, cuts=(), held_as=jnp.bfloat16):
    gain = level_of(own_key, extent, cuts, -0.22, 0.18) if cuts else 1.0
    entries = jax.random.normal(own_key, extent, jnp.float32) * scale * gain
    return jnp.minimum(jnp.maximum(entries, -most), most).astype(held_as)


def setup_inputs(seed: int = 0) -> dict:
    key_list = jax.random.split(jax.random.key(seed), 7)
    return {
        "eddy_cells": draw_eddy_cells(jax.random.fold_in(key_list[6], 71), 0),
        "eddy_signs": draw_eddy_signs(jax.random.fold_in(key_list[6], 71), 0),
        "eddy_counts": draw_eddy_counts(jax.random.fold_in(key_list[6], 71), 0),
        "stress_diag": jnp.clip(jnp.exp(math.log(3.0) - 2.3025851 * jax.random.uniform(key_list[3], (3, NY), jnp.float32) ** level_of(key_list[3], (3, NY), ((1, 16),), -0.2, 0.2)), 0.3, 3.0),
        "stress_shear": normal_values(key_list[4], (3, NY), 0.5, 3.0, ((1, 16),), jnp.float32),
        "mean_flow": normal_values(key_list[5], (3, NY, NZ), 1.0, 6.0, ((1, 16), (2, 8)), jnp.float32),
    }


shape_peak = math.sqrt(1.5)

def profile(offsets):
    return shape_peak * jnp.maximum(1.0 - jnp.abs(offsets).astype(jnp.float32) / HALF, 0.0)

def tile_field(positions, signs_here, live_count, row_anchor, col_anchor, block_count):
    block_size = min(256, CAP)
    ext_rows = TY + 2 * HALF
    ext_cols = TZ + 2 * HALF
    row_cells = row_anchor - HALF + jnp.arange(ext_rows, dtype=jnp.int32)
    col_cells = col_anchor - HALF + jnp.arange(ext_cols, dtype=jnp.int32)

    def add_block(block_index, running):
        first_slot = (block_index * block_size).astype(jnp.int32)
        slot_index = first_slot + jnp.arange(block_size, dtype=jnp.int32)
        places = lax.dynamic_slice_in_dim(positions, first_slot, block_size, 1)
        weights = lax.dynamic_slice_in_dim(signs_here, first_slot, block_size, 1).astype(jnp.float32)
        weights = weights * (slot_index < live_count).astype(jnp.float32)[None, :]
        wall_profile = profile(row_cells[:, None] - places[0][None, :])
        span_profile = profile(col_cells[:, None] - places[1][None, :])
        signed = (weights[:, None, :] * wall_profile[None, :, :]).reshape(3 * ext_rows, block_size)
        return running + lax.dot_general(signed, span_profile, (((1,), (1,)), ((), ())), precision=lax.Precision.HIGHEST, preferred_element_type=jnp.float32)
    initial = jnp.zeros((3 * ext_rows, ext_cols), jnp.float32)
    return lax.fori_loop(jnp.int32(0), block_count, add_block, initial).reshape(3, ext_rows, ext_cols)

def rescale(raw_field, stress_diag, stress_shear, mean_flow, amplitude):
    streamwise = stress_diag[0][:, None] * raw_field[0]
    normal_part = stress_shear[0][:, None] * raw_field[0] + stress_diag[1][:, None] * raw_field[1]
    spanwise = stress_shear[1][:, None] * raw_field[0] + stress_shear[2][:, None] * raw_field[1] + stress_diag[2][:, None] * raw_field[2]
    return mean_flow + amplitude * jnp.stack([streamwise, normal_part, spanwise])

def reference(eddy_cells, eddy_signs, eddy_counts, stress_diag, stress_shear, mean_flow):
    block_count = CAP // min(256, CAP)
    canvas_init = jnp.zeros((3, NY + 2 * HALF, NZ + 2 * HALF), jnp.float32)

    def add_tile(tile_index, canvas):
        tile_row = (tile_index // TILES_Z).astype(jnp.int32)
        tile_col = (tile_index % TILES_Z).astype(jnp.int32)
        positions = lax.dynamic_index_in_dim(lax.dynamic_index_in_dim(eddy_cells, tile_row, 0, False), tile_col, 0, False)
        signs_here = lax.dynamic_index_in_dim(lax.dynamic_index_in_dim(eddy_signs, tile_row, 0, False), tile_col, 0, False)
        live_count = lax.dynamic_index_in_dim(lax.dynamic_index_in_dim(eddy_counts, tile_row, 0, False), tile_col, 0, False)
        extended = tile_field(positions, signs_here, live_count, tile_row * TY, tile_col * TZ, block_count)
        anchor = (jnp.int32(0), (tile_row * TY).astype(jnp.int32), (tile_col * TZ).astype(jnp.int32))
        current = lax.dynamic_slice(canvas, anchor, extended.shape)
        return lax.dynamic_update_slice(canvas, current + extended, anchor)
    canvas = lax.fori_loop(jnp.int32(0), jnp.int32(TILES_Y * TILES_Z), add_tile, canvas_init)
    inside = canvas[:, HALF:HALF + NY, :]
    middle = inside[:, :, HALF:HALF + NZ]
    middle = middle.at[:, :, :HALF].add(inside[:, :, NZ + HALF:])
    middle = middle.at[:, :, NZ - HALF:].add(inside[:, :, :HALF])
    eddy_total = jnp.sum(eddy_counts).astype(jnp.float32)
    amplitude = jnp.sqrt(NY * NZ / (HALF * HALF) / eddy_total)
    return rescale(middle, stress_diag, stress_shear, mean_flow, amplitude)
```

```python
import jax
import jax.numpy as jnp
from jax import lax
from jax.experimental import pallas as pl
from jax.experimental.pallas import tpu as pltpu
from jax.sharding import PartitionSpec as P

TY = 2048
TZ = 256
CAP = 2048
HALF = 128
GY = 16
GZ = 8
ROWS = CAP // 128
BLOCK = 256
BLOCKS = TY // BLOCK
DEAD = 1 << 22
MESH = pl.DeviceIdType.MESH
OFFSETS = tuple((di, dj) for di in (-1, 0, 1) for dj in (-1, 0, 1))
OWN = 4


def sort_keys(vregs):
    lane = lax.broadcasted_iota(jnp.int32, (8, 128), 1)
    row = lax.broadcasted_iota(jnp.int32, (8, 128), 0)
    index = row * 128 + lane
    bits = CAP.bit_length() - 1
    for up in range(1, bits + 1):
        for step in range(up - 1, -1, -1):
            if step == 10:
                vregs = [
                    (jnp.minimum(low, high), jnp.maximum(low, high)) for low, high in vregs
                ]
                continue
            own_bit = lax.shift_right_logical(index, step) & 1
            lower = own_bit == 0
            axis, size, by = (1, 128, 1 << step) if step < 7 else (0, 8, 1 << (step - 7))
            sorted_lists = []
            for halves in vregs:
                done = []
                for half, x in enumerate(halves):
                    if up < 10:
                        take_min = ((lax.shift_right_logical(index, up) & 1) ^ own_bit) == 0
                    elif up == 10 and half == 1:
                        take_min = own_bit == 1
                    else:
                        take_min = lower
                    ahead = pltpu.roll(x, size - by, axis)
                    if 2 * by == size:
                        other = ahead
                    else:
                        other = jnp.where(lower, ahead, pltpu.roll(x, by, axis))
                    done.append(
                        jnp.where(take_min, jnp.minimum(x, other), jnp.maximum(x, other))
                    )
                sorted_lists.append(tuple(done))
            vregs = sorted_lists
    return vregs


def exchange(
    cells,
    signs,
    count,
    lists,
    bounds,
    total,
    places,
    stage,
    arrived,
    part1,
    got1,
    part2,
    got2,
    send_sem,
    recv_sem,
    send1,
    recv1,
    send2,
    recv2,
):
    gy = lax.axis_index("gy")
    gz = lax.axis_index("gz")
    barrier = pltpu.get_barrier_semaphore()

    def at(di, dj):
        return (lax.rem(gy + di + GY, GY), lax.rem(gz + dj + GZ, GZ))

    partners = [at(0, d) for d in range(1, GZ)] + [at(d, 0) for d in range(1, GY)]
    partners += [at(di, dj) for di, dj in OFFSETS if di and dj]
    for partner in partners:
        pl.semaphore_signal(barrier, inc=1, device_id=partner, device_id_type=MESH)

    live_count = count[0, 0]
    part1[...] = jnp.full((8, 128), live_count, jnp.int32).astype(jnp.float32)
    for r in range(ROWS):
        for k in range(2):
            places[k, r : r + 1, :] = cells[k : k + 1, 128 * r : 128 * r + 128]
    lane = lax.broadcasted_iota(jnp.int32, (8, 128), 1)
    row = lax.broadcasted_iota(jnp.int32, (8, 128), 0)
    keys = [[], [], []]
    for half in range(2):
        rows = slice(8 * half, 8 * half + 8)
        wall = places[0, rows, :] & (TY - 1)
        span = places[1, rows, :] & (TZ - 1)
        key = wall * 2048 + span * 8
        for c in range(3):
            key = key + lax.shift_right_logical(signs[c, rows, :] + 1, 1) * (1 << c)
        live = row * 128 + lane + 1024 * half < live_count
        key = jnp.where(live, key, DEAD)
        keys[0].append(key)
        keys[1].append(jnp.where(span < HALF - 1, key, DEAD))
        keys[2].append(jnp.where(span > HALF, key, DEAD))
    for kind, halves in enumerate(sort_keys([tuple(k) for k in keys])):
        for half, key in enumerate(halves):
            rows = slice(8 * half, 8 * half + 8)
            stage[kind, 0, rows, :] = lax.shift_right_logical(key, 11).astype(jnp.float32)
            stage[kind, 1, rows, :] = (lax.shift_right_logical(key, 3) & 255).astype(jnp.float32)
            live = key < DEAD
            for c in range(3):
                sign = (lax.shift_right_logical(key, c) & 1) * 2 - 1
                stage[kind, 2 + c, rows, :] = jnp.where(live, sign, 0).astype(jnp.float32)

    pl.semaphore_wait(barrier, len(partners))

    first = []
    for d in range(1, GZ):
        copy = pltpu.make_async_remote_copy(
            src_ref=part1,
            dst_ref=got1.at[d - 1],
            send_sem=send1.at[d - 1],
            recv_sem=recv1.at[d - 1],
            device_id=at(0, d),
            device_id_type=MESH,
        )
        copy.start()
        first.append(copy)
    sends = []
    for slot, (di, dj) in enumerate(OFFSETS):
        if di == 0 and dj == 0:
            continue
        copy = pltpu.make_async_remote_copy(
            src_ref=stage.at[{0: 0, 1: 1, -1: 2}[dj]],
            dst_ref=arrived.at[slot],
            send_sem=send_sem.at[slot],
            recv_sem=recv_sem.at[slot],
            device_id=at(-di, -dj),
            device_id_type=MESH,
        )
        copy.start()
        sends.append((slot, copy))
    for copy in first:
        copy.wait()
    mine = part1[...]
    for d in range(GZ - 1):
        mine = mine + got1[d]
    part2[...] = mine
    second = []
    for d in range(1, GY):
        copy = pltpu.make_async_remote_copy(
            src_ref=part2,
            dst_ref=got2.at[d - 1],
            send_sem=send2.at[d - 1],
            recv_sem=recv2.at[d - 1],
            device_id=at(d, 0),
            device_id_type=MESH,
        )
        copy.start()
        second.append(copy)

    lane16 = lax.broadcasted_iota(jnp.int32, (ROWS, 128), 1)

    def finish(slot, table):
        di, _ = OFFSETS[slot]
        lists[slot] = table[...]
        wall = table[0]
        starts = jnp.broadcast_to(wall[:, 0:1], (ROWS, 128))
        ends = jnp.broadcast_to(wall[:, 127:128], (ROWS, 128))
        low = (lane16 * BLOCK - (HALF - 1) - TY * di).astype(jnp.float32)
        high = jnp.minimum(
            (lane16 - BLOCKS) * BLOCK + (BLOCK + HALF - 2) - TY * di, TY - 1
        ).astype(jnp.float32)
        before = jnp.where(ends < low, 1.0, 0.0)
        begun = jnp.where(starts <= high, 1.0, 0.0)
        counted = jnp.sum(jnp.where(lane16 < BLOCKS, before, begun), axis=0, keepdims=True)
        if di:
            inside = jnp.logical_and(gy + di >= 0, gy + di < GY)
            counted = counted * jnp.where(inside, 1.0, 0.0)
        bounds[slot : slot + 1, :] = counted.astype(jnp.int32)

    finish(OWN, stage.at[0])
    for slot, copy in sends:
        copy.wait()
        finish(slot, arrived.at[slot])
    for copy in second:
        copy.wait()
    everything = part2[...]
    for d in range(GY - 1):
        everything = everything + got2[d]
    total[...] = everything


def tent(place, rows, first):
    bf = jnp.bfloat16
    y = (lax.broadcasted_iota(jnp.int32, (rows, 128), 0) + first).astype(jnp.float32).astype(bf)
    near = jnp.minimum(jnp.maximum(place, -256.0), 256.0).astype(bf)
    return jnp.maximum(bf(HALF) - jnp.abs(y - near), bf(0))


def evaluate(
    bounds, total, lists, diag, shear, mean, out, buffer, acc, scales, in_sem, out_sem
):
    def load(b):
        rows = pl.ds(pl.multiple_of(b * BLOCK, BLOCK), BLOCK)
        return pltpu.make_async_copy(mean.at[:, rows, :], buffer.at[:, rows, :], in_sem.at[b])

    def save(b):
        rows = pl.ds(pl.multiple_of(b * BLOCK, BLOCK), BLOCK)
        return pltpu.make_async_copy(buffer.at[:, rows, :], out.at[:, rows, :], out_sem.at[b])

    for b in range(BLOCKS):
        load(b).start()
    gain = jnp.sqrt(TY * GY * (TZ * GZ) / (HALF * HALF) / total[0:1, 0:1]) * (1.5 / (HALF * HALF))
    scales[0:3, :] = diag[...] * gain
    scales[3:6, :] = shear[...] * gain
    scales[6:8, :] = jnp.zeros((2, TY), jnp.float32)

    def add_list(slot, b):
        di, dj = OFFSETS[slot]
        begin, end = bounds[slot, b], bounds[slot, BLOCKS + b]
        anchor = (128 + b * BLOCK - TY * di).astype(jnp.float32)

        def pair(step, carry):
            r = begin + 2 * step
            left, right = [], []
            for part in range(2):
                chunk = r if part == 0 else jnp.minimum(r + 1, ROWS - 1)
                here = pl.ds(chunk, 1)
                left.append(tent(lists[slot, 0, here, :] - anchor, BLOCK, -128))
                q = lists[slot, 1, here, :] - 128.0 + TZ * dj
                if dj == 0:
                    shape = tent(q, TZ, -128)
                else:
                    shape = tent(q, HALF, -128 if dj < 0 else 0)
                signed = []
                for c in range(3):
                    s = lists[slot, 2 + c, here, :]
                    if part == 1:
                        s = s * jnp.where(r + 1 < ROWS, 1.0, 0.0)
                    signed.append(shape * s.astype(jnp.bfloat16))
                right.append(jnp.concatenate(signed, axis=0))
            product = lax.dot_general(
                jnp.concatenate(left, axis=1),
                jnp.concatenate(right, axis=1),
                (((1,), (1,)), ((), ())),
                preferred_element_type=jnp.float32,
            )
            if dj == 0:
                acc[...] += product
            else:
                for c in range(3):
                    at = c * TZ + (0 if dj < 0 else HALF)
                    acc[:, at : at + HALF] += product[:, c * HALF : (c + 1) * HALF]
            return carry

        lax.fori_loop(0, (end - begin + 1) // 2, pair, 0)

    @pl.loop(0, BLOCKS)
    def _(b):
        acc[...] = jnp.zeros_like(acc)
        for slot in (4, 3, 5):
            add_list(slot, b)

        @pl.when(b == 0)
        def _():
            for slot in (0, 1, 2):
                add_list(slot, b)

        @pl.when(b == BLOCKS - 1)
        def _():
            for slot in (6, 7, 8):
                add_list(slot, b)

        rows = pl.ds(pl.multiple_of(b * BLOCK, BLOCK), BLOCK)
        k = scales[:, rows].T
        raw = [acc[:, c * TZ : (c + 1) * TZ] for c in range(3)]
        load(b).wait()
        buffer[0, rows, :] += k[:, 0:1] * raw[0]
        buffer[1, rows, :] += k[:, 3:4] * raw[0] + k[:, 1:2] * raw[1]
        buffer[2, rows, :] += k[:, 4:5] * raw[0] + k[:, 5:6] * raw[1] + k[:, 2:3] * raw[2]
        save(b).start()

    for b in range(BLOCKS):
        save(b).wait()


def body(eddy_cells, eddy_signs, eddy_counts, stress_diag, stress_shear, mean_flow):
    vmem = pl.BlockSpec(memory_space=pltpu.VMEM)
    smem = pl.BlockSpec(memory_space=pltpu.SMEM)
    anywhere = pl.BlockSpec(memory_space=pl.ANY)
    dma = pltpu.SemaphoreType.DMA
    f32 = jnp.float32
    lists, bounds, total = pl.pallas_call(
        exchange,
        out_shape=(
            jax.ShapeDtypeStruct((9, 5, ROWS, 128), f32),
            jax.ShapeDtypeStruct((16, 128), jnp.int32),
            jax.ShapeDtypeStruct((8, 128), f32),
        ),
        in_specs=[vmem, vmem, smem],
        out_specs=(vmem, vmem, vmem),
        scratch_shapes=[
            pltpu.VMEM((2, ROWS, 128), jnp.int32),
            pltpu.VMEM((3, 5, ROWS, 128), f32),
            pltpu.VMEM((9, 5, ROWS, 128), f32),
            pltpu.VMEM((8, 128), f32),
            pltpu.VMEM((GZ - 1, 8, 128), f32),
            pltpu.VMEM((8, 128), f32),
            pltpu.VMEM((GY - 1, 8, 128), f32),
            dma((9,)),
            dma((9,)),
            dma((GZ - 1,)),
            dma((GZ - 1,)),
            dma((GY - 1,)),
            dma((GY - 1,)),
        ],
        compiler_params=pltpu.CompilerParams(collective_id=0, has_side_effects=True),
        name="exchange",
    )(
        eddy_cells.reshape(2, CAP),
        eddy_signs.reshape(3, ROWS, 128),
        eddy_counts,
    )
    return pl.pallas_call(
        evaluate,
        out_shape=jax.ShapeDtypeStruct((3, TY, TZ), f32),
        in_specs=[smem, vmem, vmem, vmem, vmem, anywhere],
        out_specs=anywhere,
        scratch_shapes=[
            pltpu.VMEM((3, TY, TZ), f32),
            pltpu.VMEM((BLOCK, 3 * TZ), f32),
            pltpu.VMEM((8, TY), f32),
            dma((BLOCKS,)),
            dma((BLOCKS,)),
        ],
        name="evaluate",
    )(bounds, total, lists, stress_diag, stress_shear, mean_flow)


def solution(mesh):
    return jax.shard_map(
        body,
        mesh=mesh,
        in_specs=(
            P("gy", "gz", None, None),
            P("gy", "gz", None, None),
            P("gy", "gz"),
            P(None, "gy"),
            P(None, "gy"),
            P(None, "gy", "gz"),
        ),
        out_specs=P(None, "gy", "gz"),
        check_vma=False,
    )
```

```python
import jax
import jax.numpy as jnp
from jax import lax
from jax.experimental import pallas as pl
from jax.experimental.pallas import tpu as pltpu
from jax.sharding import PartitionSpec as P

TY = 2048
TZ = 256
CAP = 2048
HALF = 128
GY = 16
GZ = 8
ROWS = CAP // 128
BLOCK = 256
BLOCKS = TY // BLOCK
DEAD = 1 << 22
MESH = pl.DeviceIdType.MESH
OFFSETS = tuple((di, dj) for di in (-1, 0, 1) for dj in (-1, 0, 1))
OWN = 4
CHUNKS = {-1: 3, 0: 5, 1: 3}


def sort_keys(vregs):
    lane = lax.broadcasted_iota(jnp.int32, (8, 128), 1)
    row = lax.broadcasted_iota(jnp.int32, (8, 128), 0)
    index = row * 128 + lane
    bits = CAP.bit_length() - 1
    for up in range(1, bits + 1):
        for step in range(up - 1, -1, -1):
            if step == 10:
                vregs = [
                    (jnp.minimum(low, high), jnp.maximum(low, high)) for low, high in vregs
                ]
                continue
            own_bit = lax.shift_right_logical(index, step) & 1
            lower = own_bit == 0
            axis, size, by = (1, 128, 1 << step) if step < 7 else (0, 8, 1 << (step - 7))
            sorted_lists = []
            for halves in vregs:
                done = []
                for half, x in enumerate(halves):
                    if up < 10:
                        take_min = ((lax.shift_right_logical(index, up) & 1) ^ own_bit) == 0
                    elif up == 10 and half == 1:
                        take_min = own_bit == 1
                    else:
                        take_min = lower
                    ahead = pltpu.roll(x, size - by, axis)
                    if 2 * by == size:
                        other = ahead
                    else:
                        other = jnp.where(lower, ahead, pltpu.roll(x, by, axis))
                    done.append(
                        jnp.where(take_min, jnp.minimum(x, other), jnp.maximum(x, other))
                    )
                sorted_lists.append(tuple(done))
            vregs = sorted_lists
    return vregs


def exchange(
    cells,
    signs,
    count,
    lists,
    bounds,
    total,
    places,
    stage,
    arrived,
    part1,
    got1,
    part2,
    got2,
    send_sem,
    recv_sem,
    send1,
    recv1,
    send2,
    recv2,
):
    gy = lax.axis_index("gy")
    gz = lax.axis_index("gz")
    barrier = pltpu.get_barrier_semaphore()

    def at(di, dj):
        return (lax.rem(gy + di + GY, GY), lax.rem(gz + dj + GZ, GZ))

    partners = [at(0, d) for d in range(1, GZ)] + [at(d, 0) for d in range(1, GY)]
    partners += [at(di, dj) for di, dj in OFFSETS if di and dj]
    for partner in partners:
        pl.semaphore_signal(barrier, inc=1, device_id=partner, device_id_type=MESH)

    live_count = count[0, 0]
    part1[...] = jnp.full((8, 128), live_count, jnp.int32).astype(jnp.float32)
    for r in range(ROWS):
        for k in range(2):
            places[k, r : r + 1, :] = cells[k : k + 1, 128 * r : 128 * r + 128]
    lane = lax.broadcasted_iota(jnp.int32, (8, 128), 1)
    row = lax.broadcasted_iota(jnp.int32, (8, 128), 0)
    keys = [[], [], []]
    for half in range(2):
        rows = slice(8 * half, 8 * half + 8)
        wall = places[0, rows, :] & (TY - 1)
        span = places[1, rows, :] & (TZ - 1)
        key = wall * 2048 + span * 8
        for c in range(3):
            key = key + lax.shift_right_logical(signs[c, rows, :] + 1, 1) * (1 << c)
        live = row * 128 + lane + 1024 * half < live_count
        key = jnp.where(live, key, DEAD)
        keys[0].append(key)
        keys[1].append(jnp.where(span < HALF - 1, key, DEAD))
        keys[2].append(jnp.where(span > HALF, key, DEAD))
    for kind, halves in enumerate(sort_keys([tuple(k) for k in keys])):
        for half, key in enumerate(halves):
            rows = slice(8 * half, 8 * half + 8)
            stage[kind, 0, rows, :] = lax.shift_right_logical(key, 11).astype(jnp.float32)
            stage[kind, 1, rows, :] = (lax.shift_right_logical(key, 3) & 255).astype(jnp.float32)
            live = key < DEAD
            for c in range(3):
                sign = (lax.shift_right_logical(key, c) & 1) * 2 - 1
                stage[kind, 2 + c, rows, :] = jnp.where(live, sign, 0).astype(jnp.float32)

    pl.semaphore_wait(barrier, len(partners))

    first = []
    for d in range(1, GZ):
        copy = pltpu.make_async_remote_copy(
            src_ref=part1,
            dst_ref=got1.at[d - 1],
            send_sem=send1.at[d - 1],
            recv_sem=recv1.at[d - 1],
            device_id=at(0, d),
            device_id_type=MESH,
        )
        copy.start()
        first.append(copy)
    sends = []
    for slot, (di, dj) in enumerate(OFFSETS):
        if di == 0 and dj == 0:
            continue
        copy = pltpu.make_async_remote_copy(
            src_ref=stage.at[{0: 0, 1: 1, -1: 2}[dj]],
            dst_ref=arrived.at[slot],
            send_sem=send_sem.at[slot],
            recv_sem=recv_sem.at[slot],
            device_id=at(-di, -dj),
            device_id_type=MESH,
        )
        copy.start()
        sends.append((slot, copy))
    for copy in first:
        copy.wait()
    mine = part1[...]
    for d in range(GZ - 1):
        mine = mine + got1[d]
    part2[...] = mine
    second = []
    for d in range(1, GY):
        copy = pltpu.make_async_remote_copy(
            src_ref=part2,
            dst_ref=got2.at[d - 1],
            send_sem=send2.at[d - 1],
            recv_sem=recv2.at[d - 1],
            device_id=at(d, 0),
            device_id_type=MESH,
        )
        copy.start()
        second.append(copy)

    lane16 = lax.broadcasted_iota(jnp.int32, (ROWS, 128), 1)

    def finish(slot, table):
        di, _ = OFFSETS[slot]
        lists[slot] = table[...]
        wall = table[0]
        starts = jnp.broadcast_to(wall[:, 0:1], (ROWS, 128))
        ends = jnp.broadcast_to(wall[:, 127:128], (ROWS, 128))
        low = (lane16 * BLOCK - (HALF - 1) - TY * di).astype(jnp.float32)
        high = jnp.minimum(
            (lane16 - BLOCKS) * BLOCK + (BLOCK + HALF - 2) - TY * di, TY - 1
        ).astype(jnp.float32)
        before = jnp.where(ends < low, 1.0, 0.0)
        begun = jnp.where(starts <= high, 1.0, 0.0)
        counted = jnp.sum(jnp.where(lane16 < BLOCKS, before, begun), axis=0, keepdims=True)
        if di:
            inside = jnp.logical_and(gy + di >= 0, gy + di < GY)
            counted = counted * jnp.where(inside, 1.0, 0.0)
        bounds[slot : slot + 1, :] = counted.astype(jnp.int32)

    finish(OWN, stage.at[0])
    for slot, copy in sends:
        copy.wait()
        finish(slot, arrived.at[slot])
    for copy in second:
        copy.wait()
    everything = part2[...]
    for d in range(GY - 1):
        everything = everything + got2[d]
    total[...] = everything


def tent(place, rows, first):
    bf = jnp.bfloat16
    y = (lax.broadcasted_iota(jnp.int32, (rows, 128), 0) + first).astype(jnp.float32).astype(bf)
    near = jnp.minimum(jnp.maximum(place, -256.0), 256.0).astype(bf)
    return jnp.maximum(bf(HALF) - jnp.abs(y - near), bf(0))


def evaluate(
    bounds, total, lists, diag, shear, mean, out, buffer, acc, scales, in_sem, out_sem
):
    bf = jnp.bfloat16

    def load(b):
        rows = pl.ds(pl.multiple_of(b * BLOCK, BLOCK), BLOCK)
        return pltpu.make_async_copy(mean.at[:, rows, :], buffer.at[:, rows, :], in_sem.at[b])

    def save(b):
        rows = pl.ds(pl.multiple_of(b * BLOCK, BLOCK), BLOCK)
        return pltpu.make_async_copy(buffer.at[:, rows, :], out.at[:, rows, :], out_sem.at[b])

    for b in range(BLOCKS):
        load(b).start()
    gain = jnp.sqrt(TY * GY * (TZ * GZ) / (HALF * HALF) / total[0:1, 0:1]) * (1.5 / (HALF * HALF))
    scales[0:3, :] = diag[...] * gain
    scales[3:6, :] = shear[...] * gain
    scales[6:8, :] = jnp.zeros((2, TY), jnp.float32)

    def chunk_counts(dj, b):
        slots = [(di + 1) * 3 + dj + 1 for di in (-1, 0, 1)]
        begins = [bounds[slot, b] for slot in slots]
        numbers = [
            jnp.maximum(bounds[slot, BLOCKS + b] - begin, 0) for slot, begin in zip(slots, begins)
        ]
        return begins, numbers

    def product(dj, b, begins, numbers, start, chunks):
        left, right = [], []
        above = numbers[0]
        beside = above + numbers[1]
        every = beside + numbers[2]
        for part in range(chunks):
            i = start + part
            di = jnp.where(i < above, 0, jnp.where(i < beside, 1, 2))
            base = jnp.where(
                i < above,
                begins[0],
                jnp.where(i < beside, begins[1] - above, begins[2] - beside),
            )
            used = i < every
            slot = jnp.where(used, di * 3 + dj + 1, 0)
            chunk = pl.ds(jnp.where(used, base + i, 0), 1)
            live = jnp.where(used, 1.0, 0.0)
            anchor = (128 + b * BLOCK - TY * (di - 1)).astype(jnp.float32)
            left.append(tent(lists[slot, 0, chunk, :] - anchor, BLOCK, -128))
            q = lists[slot, 1, chunk, :] - 128.0 + TZ * dj
            if dj == 0:
                shape = tent(q, TZ, -128)
            else:
                shape = tent(q, HALF, -128 if dj < 0 else 0)
            right.append(
                jnp.concatenate(
                    [shape * (lists[slot, 2 + c, chunk, :] * live).astype(bf) for c in range(3)],
                    axis=0,
                )
            )
        return lax.dot_general(
            jnp.concatenate(left, axis=1),
            jnp.concatenate(right, axis=1),
            (((1,), (1,)), ((), ())),
            preferred_element_type=jnp.float32,
        )

    def accumulate(b, side):
        ranges = {dj: chunk_counts(dj, b) for dj in (-1, 0, 1)}
        parts = {dj: product(dj, b, *ranges[dj], 0, CHUNKS[dj]) for dj in (-1, 0, 1)}
        for c in range(3):
            for half, dj in ((0, -1), (1, 1)):
                at = c * TZ + half * HALF
                acc[side, :, at : at + HALF] = (
                    parts[0][:, at : at + HALF] + parts[dj][:, c * HALF : (c + 1) * HALF]
                )
        return ranges

    def overflow(b, side, ranges):
        for dj in (-1, 0, 1):
            begins, numbers = ranges[dj]
            chunks = CHUNKS[dj]

            def more(step, carry, dj=dj, begins=begins, numbers=numbers, chunks=chunks):
                extra = product(dj, b, begins, numbers, step * chunks, chunks)
                if dj == 0:
                    acc[side] += extra
                else:
                    for c in range(3):
                        at = c * TZ + (0 if dj < 0 else HALF)
                        acc[side, :, at : at + HALF] += extra[:, c * HALF : (c + 1) * HALF]
                return carry

            count = numbers[0] + numbers[1] + numbers[2]
            lax.fori_loop(1, (count + chunks - 1) // chunks, more, 0)

    def finish(b, side):
        rows = pl.ds(pl.multiple_of(b * BLOCK, BLOCK), BLOCK)
        k = scales[:, rows].T
        raw = [acc[side, :, c * TZ : (c + 1) * TZ] for c in range(3)]
        buffer[0, rows, :] += k[:, 0:1] * raw[0]
        buffer[1, rows, :] += k[:, 3:4] * raw[0] + k[:, 1:2] * raw[1]
        buffer[2, rows, :] += k[:, 4:5] * raw[0] + k[:, 5:6] * raw[1] + k[:, 2:3] * raw[2]
        save(b).start()

    overflow(jnp.int32(0), 0, accumulate(jnp.int32(0), 0))

    @pl.loop(0, BLOCKS // 2 - 1)
    def _(twice):
        for side in (1, 0):
            b = 2 * twice + 2 - side
            load(b - 1).wait()
            ranges = accumulate(b, side)
            finish(b - 1, 1 - side)
            overflow(b, side, ranges)

    b = jnp.int32(BLOCKS - 1)
    load(b - 1).wait()
    ranges = accumulate(b, 1)
    finish(b - 1, 0)
    overflow(b, 1, ranges)
    load(b).wait()
    finish(b, 1)
    for b in range(BLOCKS):
        save(b).wait()


def body(eddy_cells, eddy_signs, eddy_counts, stress_diag, stress_shear, mean_flow):
    vmem = pl.BlockSpec(memory_space=pltpu.VMEM)
    smem = pl.BlockSpec(memory_space=pltpu.SMEM)
    anywhere = pl.BlockSpec(memory_space=pl.ANY)
    dma = pltpu.SemaphoreType.DMA
    f32 = jnp.float32
    lists, bounds, total = pl.pallas_call(
        exchange,
        out_shape=(
            jax.ShapeDtypeStruct((9, 5, ROWS, 128), f32),
            jax.ShapeDtypeStruct((16, 128), jnp.int32),
            jax.ShapeDtypeStruct((8, 128), f32),
        ),
        in_specs=[vmem, vmem, smem],
        out_specs=(vmem, vmem, vmem),
        scratch_shapes=[
            pltpu.VMEM((2, ROWS, 128), jnp.int32),
            pltpu.VMEM((3, 5, ROWS, 128), f32),
            pltpu.VMEM((9, 5, ROWS, 128), f32),
            pltpu.VMEM((8, 128), f32),
            pltpu.VMEM((GZ - 1, 8, 128), f32),
            pltpu.VMEM((8, 128), f32),
            pltpu.VMEM((GY - 1, 8, 128), f32),
            dma((9,)),
            dma((9,)),
            dma((GZ - 1,)),
            dma((GZ - 1,)),
            dma((GY - 1,)),
            dma((GY - 1,)),
        ],
        compiler_params=pltpu.CompilerParams(collective_id=0, has_side_effects=True),
        name="exchange",
    )(
        eddy_cells.reshape(2, CAP),
        eddy_signs.reshape(3, ROWS, 128),
        eddy_counts,
    )
    return call_evaluate(bounds, total, lists, stress_diag, stress_shear, mean_flow)


def call_evaluate(bounds, total, lists, stress_diag, stress_shear, mean_flow):
    vmem = pl.BlockSpec(memory_space=pltpu.VMEM)
    smem = pl.BlockSpec(memory_space=pltpu.SMEM)
    anywhere = pl.BlockSpec(memory_space=pl.ANY)
    dma = pltpu.SemaphoreType.DMA
    f32 = jnp.float32
    return pl.pallas_call(
        evaluate,
        out_shape=jax.ShapeDtypeStruct((3, TY, TZ), f32),
        in_specs=[smem, vmem, vmem, vmem, vmem, anywhere],
        out_specs=anywhere,
        scratch_shapes=[
            pltpu.VMEM((3, TY, TZ), f32),
            pltpu.VMEM((2, BLOCK, 3 * TZ), f32),
            pltpu.VMEM((8, TY), f32),
            dma((BLOCKS,)),
            dma((BLOCKS,)),
        ],
        name="evaluate",
    )(bounds, total, lists, stress_diag, stress_shear, mean_flow)


def solution(mesh):
    return jax.shard_map(
        body,
        mesh=mesh,
        in_specs=(
            P("gy", "gz", None, None),
            P("gy", "gz", None, None),
            P("gy", "gz"),
            P(None, "gy"),
            P(None, "gy"),
            P(None, "gy", "gz"),
        ),
        out_specs=P(None, "gy", "gz"),
        check_vma=False,
    )
```

```python
import jax
import jax.numpy as jnp
from jax import lax
from jax.experimental import pallas as pl
from jax.experimental.pallas import tpu as pltpu
from jax.sharding import PartitionSpec as P

TY = 2048
TZ = 256
CAP = 2048
HALF = 128
GY = 16
GZ = 8
ROWS = CAP // 128
BLOCK = 256
BLOCKS = TY // BLOCK
DEAD = 1 << 22
VMEM_LIMIT = 36 << 20
MESH = pl.DeviceIdType.MESH
OFFSETS = tuple((di, dj) for di in (-1, 0, 1) for dj in (-1, 0, 1))
OWN = 4
SPLIT = 8
OWN_CHUNKS = 5
SIDE_CHUNKS = 3
END_CHUNKS = 2


def sort_keys(vregs):
    lane = lax.broadcasted_iota(jnp.int32, (8, 128), 1)
    row = lax.broadcasted_iota(jnp.int32, (8, 128), 0)
    index = row * 128 + lane
    bits = CAP.bit_length() - 1
    for up in range(1, bits + 1):
        for step in range(up - 1, -1, -1):
            if step == 10:
                vregs = [
                    (jnp.minimum(low, high), jnp.maximum(low, high)) for low, high in vregs
                ]
                continue
            own_bit = lax.shift_right_logical(index, step) & 1
            lower = own_bit == 0
            axis, size, by = (1, 128, 1 << step) if step < 7 else (0, 8, 1 << (step - 7))
            sorted_lists = []
            for halves in vregs:
                done = []
                for half, x in enumerate(halves):
                    if up < 10:
                        take_min = ((lax.shift_right_logical(index, up) & 1) ^ own_bit) == 0
                    elif up == 10 and half == 1:
                        take_min = own_bit == 1
                    else:
                        take_min = lower
                    ahead = pltpu.roll(x, size - by, axis)
                    if 2 * by == size:
                        other = ahead
                    else:
                        other = jnp.where(lower, ahead, pltpu.roll(x, by, axis))
                    done.append(
                        jnp.where(take_min, jnp.minimum(x, other), jnp.maximum(x, other))
                    )
                sorted_lists.append(tuple(done))
            vregs = sorted_lists
    return vregs


def exchange(
    cells_in,
    signs_in,
    count,
    mean,
    lists,
    bounds,
    total,
    own,
    held,
    places,
    stage,
    own_edges,
    own_bounds,
    list_bounds,
    bound_sem,
    arrived,
    part1,
    got1,
    part2,
    got2,
    send_sem,
    recv_sem,
    send1,
    recv1,
    send2,
    recv2,
    part3,
    got3,
    send3,
    recv3,
    mean_sem,
    cells,
    signs,
    input_sem,
):
    inputs = [
        pltpu.make_async_copy(cells_in, cells, input_sem.at[0]),
        pltpu.make_async_copy(signs_in, signs, input_sem.at[1]),
    ]
    for copy in inputs:
        copy.start()
    fetch = pltpu.make_async_copy(mean, held, mean_sem)
    fetch.start()
    gy = lax.axis_index("gy")
    gz = lax.axis_index("gz")
    barrier = pltpu.get_barrier_semaphore()

    def at(di, dj):
        return (lax.rem(gy + di + GY, GY), lax.rem(gz + dj + GZ, GZ))

    def along_y(d):
        return (gy - lax.rem(gy, 4) + lax.rem(gy + d, 4), gz)

    groups = [
        [at(0, d) for d in range(1, GZ)],
        [along_y(d) for d in range(1, 4)],
        [at(4 * d, 0) for d in range(1, 4)],
    ]
    for group in groups:
        for partner in group:
            pl.semaphore_signal(barrier, inc=1, device_id=partner, device_id_type=MESH)
    inside = {di: jnp.logical_and(gy + di >= 0, gy + di < GY) for di in (-1, 1)}
    for di in (-1, 1):

        @pl.when(inside[di])
        def _():
            for dj in (-1, 0, 1):
                pl.semaphore_signal(
                    barrier, inc=1, device_id=at(di, dj), device_id_type=MESH
                )

    live_count = count[0, 0]
    part1[...] = jnp.full((8, 128), live_count, jnp.int32).astype(jnp.float32)
    arrivals = sum(len(group) for group in groups)
    for di in (-1, 1):
        arrivals = arrivals + jnp.where(inside[di], 3, 0)
    pl.semaphore_wait(barrier, arrivals)

    def start_phase(phase):
        part, got, sent, received = phases[phase]
        copies = []
        for k, partner in enumerate(groups[phase]):
            copy = pltpu.make_async_remote_copy(
                src_ref=part,
                dst_ref=got.at[k],
                send_sem=sent.at[k],
                recv_sem=received.at[k],
                device_id=partner,
                device_id_type=MESH,
            )
            copy.start()
            copies.append(copy)
        return copies

    def end_phase(phase, copies, result):
        part, got, _, _ = phases[phase]
        for copy in copies:
            copy.wait()
        value = part[...]
        for k in range(len(copies)):
            value = value + got[k]
        result[...] = value

    phases = [
        (part1, got1, send1, recv1),
        (part2, got2, send2, recv2),
        (part3, got3, send3, recv3),
    ]
    counting = start_phase(0)

    for copy in inputs:
        copy.wait()
    for r in range(ROWS):
        for k in range(2):
            places[k, r : r + 1, :] = cells[k : k + 1, 128 * r : 128 * r + 128]
    lane = lax.broadcasted_iota(jnp.int32, (8, 128), 1)
    row = lax.broadcasted_iota(jnp.int32, (8, 128), 0)
    keys = [[], [], []]
    for half in range(2):
        rows = slice(8 * half, 8 * half + 8)
        wall = places[0, rows, :] & (TY - 1)
        span = places[1, rows, :] & (TZ - 1)
        key = wall * 2048 + span * 8
        for c in range(3):
            key = key + lax.shift_right_logical(signs[c, rows, :] + 1, 1) * (1 << c)
        live = row * 128 + lane + 1024 * half < live_count
        key = jnp.where(live, key, DEAD)
        keys[0].append(key)
        keys[1].append(jnp.where(span < HALF - 1, key, DEAD))
        keys[2].append(jnp.where(span > HALF, key, DEAD))
    for kind, halves in enumerate(sort_keys([tuple(k) for k in keys])):
        for half, key in enumerate(halves):
            rows = slice(8 * half, 8 * half + 8)
            stage[kind, 0, rows, :] = lax.shift_right_logical(key, 11)
            stage[kind, 1, rows, :] = lax.shift_right_logical(key, 3) & 255
            live = key < DEAD
            for c in range(3):
                sign = (lax.shift_right_logical(key, c) & 1) * 2 - 1
                stage[kind, 2 + c, rows, :] = jnp.where(live, sign, 0)

    sends = {}
    for slot, (di, dj) in enumerate(OFFSETS):
        if slot == OWN:
            continue
        sends[slot] = pltpu.make_async_remote_copy(
            src_ref=stage.at[{0: 0, 1: 1, -1: 2}[dj]],
            dst_ref=arrived.at[slot],
            send_sem=send_sem.at[slot],
            recv_sem=recv_sem.at[slot],
            device_id=at(-di, -dj),
            device_id_type=MESH,
        )
    for dj in (-1, 1):
        sends[4 + dj].start()
    for di in (-1, 1):

        @pl.when(inside[-di])
        def _():
            for dj in (-1, 0, 1):
                sends[4 + 3 * di + dj].start()

    lane16 = lax.broadcasted_iota(jnp.int32, (ROWS, 128), 1)

    def edges(slot, table):
        di, _ = OFFSETS[slot]
        wall = table[0]
        starts = jnp.broadcast_to(wall[:, 0:1], (ROWS, 128))
        ends = jnp.broadcast_to(wall[:, 127:128], (ROWS, 128))
        low = lane16 * BLOCK - (HALF - 1) - TY * di
        high = jnp.minimum(
            (lane16 - BLOCKS) * BLOCK + (BLOCK + HALF - 2) - TY * di, TY - 1
        )
        before = jnp.where(ends < low, 1, 0)
        begun = jnp.where(starts <= high, 1, 0)
        return jnp.sum(jnp.where(lane16 < BLOCKS, before, begun), axis=0, keepdims=True)

    own_edges[...] = jnp.broadcast_to(edges(OWN, stage.at[0]), (8, 128))
    lists[OWN] = stage[0]
    to_scalars = pltpu.make_async_copy(own_edges, own_bounds, bound_sem.at[0])
    to_scalars.start()
    end_phase(0, counting, part2)
    counting = start_phase(1)
    to_scalars.wait()

    def own_block(b):
        begin = own_bounds[0, b]
        number = jnp.maximum(own_bounds[0, BLOCKS + b] - begin, 0)
        own[b] = product(lists, 0, b, [0, begin, 0], [0, number, 0], 0, OWN_CHUNKS)

    pl.loop(0, SPLIT)(own_block)
    end_phase(1, counting, part3)
    counting = start_phase(2)
    pl.loop(SPLIT, BLOCKS)(own_block)

    bounds[OWN : OWN + 1, :] = own_edges[0:1, :]

    def finish(slot):
        lists[slot] = arrived[slot]
        bounds[slot : slot + 1, :] = edges(slot, arrived.at[slot])

    for dj in (-1, 1):
        sends[4 + dj].wait()
        finish(4 + dj)
    for di in (-1, 1):

        @pl.when(inside[-di])
        def _():
            for dj in (-1, 0, 1):
                sends[4 + 3 * di + dj].wait_send()

        @pl.when(inside[di])
        def _():
            for dj in (-1, 0, 1):
                slot = 4 + 3 * di + dj
                sends[slot].wait_recv()
                finish(slot)

        @pl.when(jnp.logical_not(inside[di]))
        def _():
            for dj in (-1, 0, 1):
                slot = 4 + 3 * di + dj
                lists[slot] = jnp.zeros((5, ROWS, 128), jnp.int32)
                bounds[slot : slot + 1, :] = jnp.zeros((1, 128), jnp.int32)

    bounds[9:16, :] = jnp.zeros((7, 128), jnp.int32)
    to_scalars = pltpu.make_async_copy(bounds, list_bounds, bound_sem.at[1])
    to_scalars.start()
    to_scalars.wait()

    def side_block(b):
        parts = {
            dj: product(lists, dj, b, *chunk_counts(list_bounds, dj, b), 0, SIDE_CHUNKS)
            for dj in (-1, 1)
        }
        for c in range(3):
            for half, dj in ((0, -1), (1, 1)):
                at = c * TZ + half * HALF
                own[b, :, at : at + HALF] += parts[dj][:, c * HALF : (c + 1) * HALF]

    pl.loop(0, BLOCKS)(side_block)
    for b in (0, BLOCKS - 1):
        ranges = chunk_counts(list_bounds, 0, b)
        own[b] += product(lists, 0, jnp.int32(b), *ranges, 0, END_CHUNKS)
    end_phase(2, counting, total)
    fetch.wait()


def chunk_counts(bounds, dj, b):
    slots = [(di + 1) * 3 + dj + 1 for di in (-1, 0, 1)]
    begins = [bounds[slot, b] for slot in slots]
    numbers = [
        jnp.maximum(bounds[slot, BLOCKS + b] - begin, 0) for slot, begin in zip(slots, begins)
    ]
    if dj == 0:
        begins[1] = numbers[1] = 0
    return begins, numbers


def product(lists, dj, b, begins, numbers, start, chunks):
    bf = jnp.bfloat16
    left, right = [], []
    above = numbers[0]
    beside = above + numbers[1]
    every = beside + numbers[2]
    for part in range(chunks):
        i = start + part
        di = jnp.where(i < above, 0, jnp.where(i < beside, 1, 2))
        base = jnp.where(
            i < above,
            begins[0],
            jnp.where(i < beside, begins[1] - above, begins[2] - beside),
        )
        used = i < every
        slot = jnp.where(used, di * 3 + dj + 1, OWN)
        chunk = pl.ds(jnp.where(used, base + i, 0), 1)
        live = jnp.where(used, 1, 0)
        anchor = 128 + b * BLOCK - TY * (di - 1)
        left.append(tent(lists[slot, 0, chunk, :] - anchor, BLOCK, -128))
        q = lists[slot, 1, chunk, :] - 128 + TZ * dj
        if dj == 0:
            shape = tent(q, TZ, -128)
        else:
            shape = tent(q, HALF, -128 if dj < 0 else 0)
        signed = [
            shape * (lists[slot, 2 + c, chunk, :] * live).astype(jnp.float32).astype(bf)
            for c in range(3)
        ]
        right.append(jnp.concatenate(signed, axis=0))
    return lax.dot_general(
        jnp.concatenate(left, axis=1),
        jnp.concatenate(right, axis=1),
        (((1,), (1,)), ((), ())),
        preferred_element_type=jnp.float32,
    )


def tent(place, rows, first):
    bf = jnp.bfloat16
    y = (lax.broadcasted_iota(jnp.int32, (rows, 128), 0) + first).astype(jnp.float32).astype(bf)
    near = jnp.minimum(jnp.maximum(place, -256), 256).astype(jnp.float32).astype(bf)
    return jnp.maximum(bf(HALF) - jnp.abs(y - near), bf(0))


def evaluate(bounds, total, lists, diag, shear, own, mean, out, buffer, acc, scales, out_sem):
    def save(b):
        rows = pl.ds(pl.multiple_of(b * BLOCK, BLOCK), BLOCK)
        return pltpu.make_async_copy(buffer.at[:, rows, :], out.at[:, rows, :], out_sem.at[b])

    gain = jnp.sqrt(TY * GY * (TZ * GZ) / (HALF * HALF) / total[0:1, 0:1]) * (1.5 / (HALF * HALF))
    scales[0:3, :] = diag[...] * gain
    scales[3:6, :] = shear[...] * gain
    scales[6:8, :] = jnp.zeros((2, TY), jnp.float32)

    def finish(b, raw):
        rows = pl.ds(pl.multiple_of(b * BLOCK, BLOCK), BLOCK)
        k = scales[:, rows].T
        raw = [raw[:, c * TZ : (c + 1) * TZ] for c in range(3)]
        buffer[0, rows, :] = mean[0, rows, :] + k[:, 0:1] * raw[0]
        buffer[1, rows, :] = mean[1, rows, :] + k[:, 3:4] * raw[0] + k[:, 1:2] * raw[1]
        buffer[2, rows, :] = (
            mean[2, rows, :] + k[:, 4:5] * raw[0] + k[:, 5:6] * raw[1] + k[:, 2:3] * raw[2]
        )
        save(b).start()

    def leftovers(b):
        begin = bounds[OWN, b]
        number = jnp.maximum(bounds[OWN, BLOCKS + b] - begin, 0)
        jobs = [(0, [0, begin, 0], [0, number, 0], OWN_CHUNKS)]
        for dj, done in ((-1, SIDE_CHUNKS), (0, END_CHUNKS), (1, SIDE_CHUNKS)):
            jobs.append((dj, *chunk_counts(bounds, dj, b), done))
        return jobs

    @pl.loop(0, BLOCKS)
    def _(b):
        jobs = leftovers(b)
        counts = [numbers[0] + numbers[1] + numbers[2] for _, _, numbers, _ in jobs]
        some = counts[0] > jobs[0][3]
        for count, job in zip(counts[1:], jobs[1:]):
            some = jnp.logical_or(some, count > job[3])

        @pl.when(some)
        def _():
            acc[...] = own[b]
            for count, (dj, begins, numbers, done) in zip(counts, jobs):

                def more(step, carry, dj=dj, begins=begins, numbers=numbers, done=done):
                    extra = product(lists, dj, b, begins, numbers, done + step * 2, 2)
                    if dj == 0:
                        acc[...] += extra
                    else:
                        for c in range(3):
                            at = c * TZ + (0 if dj < 0 else HALF)
                            acc[:, at : at + HALF] += extra[:, c * HALF : (c + 1) * HALF]
                    return carry

                lax.fori_loop(0, jnp.maximum(count - done + 1, 0) // 2, more, 0)
            finish(b, acc)

        @pl.when(jnp.logical_not(some))
        def _():
            finish(b, own.at[b])

    for b in range(BLOCKS):
        save(b).wait()


def body(eddy_cells, eddy_signs, eddy_counts, stress_diag, stress_shear, mean_flow):
    vmem = pl.BlockSpec(memory_space=pltpu.VMEM)
    smem = pl.BlockSpec(memory_space=pltpu.SMEM)
    anywhere = pl.BlockSpec(memory_space=pl.ANY)
    hbm = pl.BlockSpec(memory_space=pltpu.HBM)
    dma = pltpu.SemaphoreType.DMA
    f32, i32 = jnp.float32, jnp.int32
    lists, bounds, total, own, held = pl.pallas_call(
        exchange,
        out_shape=(
            pltpu.VMEM((9, 5, ROWS, 128), i32),
            jax.ShapeDtypeStruct((16, 128), jnp.int32),
            pltpu.VMEM((8, 128), f32),
            pltpu.VMEM((BLOCKS, BLOCK, 3 * TZ), f32),
            pltpu.VMEM((3, TY, TZ), f32),
        ),
        in_specs=[hbm, hbm, smem, hbm],
        out_specs=(vmem, vmem, vmem, vmem, vmem),
        scratch_shapes=[
            pltpu.VMEM((2, ROWS, 128), jnp.int32),
            pltpu.VMEM((3, 5, ROWS, 128), i32),
            pltpu.VMEM((8, 128), i32),
            pltpu.SMEM((8, 128), i32),
            pltpu.SMEM((16, 128), i32),
            dma((2,)),
            pltpu.VMEM((9, 5, ROWS, 128), i32),
            pltpu.VMEM((8, 128), f32),
            pltpu.VMEM((GZ - 1, 8, 128), f32),
            pltpu.VMEM((8, 128), f32),
            pltpu.VMEM((3, 8, 128), f32),
            dma((9,)),
            dma((9,)),
            dma((GZ - 1,)),
            dma((GZ - 1,)),
            dma((3,)),
            dma((3,)),
            pltpu.VMEM((8, 128), f32),
            pltpu.VMEM((3, 8, 128), f32),
            dma((3,)),
            dma((3,)),
            dma,
            pltpu.VMEM((2, CAP), jnp.int32),
            pltpu.VMEM((3, ROWS, 128), jnp.int32),
            dma((2,)),
        ],
        compiler_params=pltpu.CompilerParams(
            collective_id=0, has_side_effects=True, vmem_limit_bytes=VMEM_LIMIT
        ),
        name="exchange",
    )(
        pltpu.with_memory_space_constraint(eddy_cells.reshape(2, CAP), pltpu.HBM),
        pltpu.with_memory_space_constraint(eddy_signs.reshape(3, ROWS, 128), pltpu.HBM),
        eddy_counts,
        mean_flow,
    )
    return pl.pallas_call(
        evaluate,
        out_shape=jax.ShapeDtypeStruct((3, TY, TZ), f32),
        in_specs=[smem, vmem, vmem, vmem, vmem, vmem, vmem],
        out_specs=anywhere,
        scratch_shapes=[
            pltpu.VMEM((3, TY, TZ), f32),
            pltpu.VMEM((BLOCK, 3 * TZ), f32),
            pltpu.VMEM((8, TY), f32),
            dma((BLOCKS,)),
        ],
        compiler_params=pltpu.CompilerParams(vmem_limit_bytes=VMEM_LIMIT),
        name="evaluate",
    )(bounds, total, lists, stress_diag, stress_shear, own, held)


def solution(mesh):
    return jax.shard_map(
        body,
        mesh=mesh,
        in_specs=(
            P("gy", "gz", None, None),
            P("gy", "gz", None, None),
            P("gy", "gz"),
            P(None, "gy"),
            P(None, "gy"),
            P(None, "gy", "gz"),
        ),
        out_specs=P(None, "gy", "gz"),
        check_vma=False,
    )
```

```python
import jax
import jax.numpy as jnp
from jax import lax
from jax.experimental import pallas as pl
from jax.experimental.pallas import tpu as pltpu
from jax.sharding import PartitionSpec as P

TY = 2048
TZ = 256
CAP = 2048
HALF = 128
GY = 16
GZ = 8
ROWS = CAP // 128
BLOCK = 256
BLOCKS = TY // BLOCK
DEAD = 1 << 22
VMEM_LIMIT = 36 << 20
MESH = pl.DeviceIdType.MESH
OFFSETS = tuple((di, dj) for di in (-1, 0, 1) for dj in (-1, 0, 1))
OWN = 4
SPLIT = 8
UNROLL_OWN = 2
UNROLL_SIDE = 2
OWN_CHUNKS = 5
SIDE_CHUNKS = 3
END_CHUNKS = 2


def sort_keys(vregs):
    lane = lax.broadcasted_iota(jnp.int32, (8, 128), 1)
    row = lax.broadcasted_iota(jnp.int32, (8, 128), 0)
    flat = [half for halves in vregs for half in halves]
    flat += [jnp.zeros((8, 128), jnp.int32)] * (16 - len(flat))
    turned = jnp.concatenate(flat, axis=0).T
    x = [turned[8 * i : 8 * i + 8, :] for i in range(16)]
    zero = {t: (lax.shift_right_logical(row, t) & 1) == 0 for t in range(3)}
    zero |= {t: (lax.shift_right_logical(lane, t - 7) & 1) == 0 for t in range(7, 11)}

    def rising(up, i):
        if up == 11:
            return True
        if 3 <= up < 7:
            return not (i >> (up - 3)) & 1
        return zero[up]

    for up in range(1, 12):
        for step in range(up - 1, -1, -1):
            new = [None] * 16
            if 3 <= step < 7:
                for i in range(16):
                    j = i ^ (1 << (step - 3))
                    if j < i:
                        continue
                    low, high = jnp.minimum(x[i], x[j]), jnp.maximum(x[i], x[j])
                    r = rising(up, i)
                    if r is True:
                        new[i], new[j] = low, high
                    elif r is False:
                        new[i], new[j] = high, low
                    else:
                        new[i], new[j] = jnp.where(r, low, high), jnp.where(r, high, low)
            else:
                axis, size, by = (0, 8, 1 << step) if step < 3 else (1, 128, 1 << (step - 7))
                lower = zero[step]
                same = None
                for i in range(16):
                    ahead = pltpu.roll(x[i], size - by, axis)
                    if 2 * by == size:
                        other = ahead
                    else:
                        other = jnp.where(lower, ahead, pltpu.roll(x[i], by, axis))
                    low, high = jnp.minimum(x[i], other), jnp.maximum(x[i], other)
                    r = rising(up, i)
                    if r is True:
                        new[i] = jnp.where(lower, low, high)
                    elif r is False:
                        new[i] = jnp.where(lower, high, low)
                    else:
                        same = lower == r if same is None else same
                        new[i] = jnp.where(same, low, high)
            x = new
    back = jnp.concatenate(x, axis=0).T
    return [(back[16 * i : 16 * i + 8, :], back[16 * i + 8 : 16 * i + 16, :]) for i in range(len(vregs))]


def exchange(
    cells_in,
    signs_in,
    count,
    diag_in,
    shear_in,
    mean,
    lists,
    bounds,
    total,
    own,
    held,
    places,
    stage,
    own_edges,
    own_bounds,
    list_bounds,
    bound_sem,
    arrived,
    part1,
    got1,
    part2,
    got2,
    send_sem,
    recv_sem,
    send1,
    recv1,
    send2,
    recv2,
    part3,
    got3,
    send3,
    recv3,
    mean_sem,
    cells,
    signs,
    input_sem,
    scales,
    diag,
    shear,
):
    inputs = [
        pltpu.make_async_copy(cells_in, cells, input_sem.at[0]),
        pltpu.make_async_copy(signs_in, signs, input_sem.at[1]),
        pltpu.make_async_copy(diag_in, diag, input_sem.at[2]),
        pltpu.make_async_copy(shear_in, shear, input_sem.at[3]),
    ]
    for copy in inputs:
        copy.start()
    fetch = pltpu.make_async_copy(mean, held, mean_sem)
    fetch.start()
    gy = lax.axis_index("gy")
    gz = lax.axis_index("gz")
    barrier = pltpu.get_barrier_semaphore()

    def at(di, dj):
        return (lax.rem(gy + di + GY, GY), lax.rem(gz + dj + GZ, GZ))

    def along_y(d):
        return (gy - lax.rem(gy, 4) + lax.rem(gy + d, 4), gz)

    groups = [
        [at(0, d) for d in range(1, GZ)],
        [along_y(d) for d in range(1, 4)],
        [at(4 * d, 0) for d in range(1, 4)],
    ]
    for group in groups:
        for partner in group:
            pl.semaphore_signal(barrier, inc=1, device_id=partner, device_id_type=MESH)
    inside = {di: jnp.logical_and(gy + di >= 0, gy + di < GY) for di in (-1, 1)}
    for di in (-1, 1):

        @pl.when(inside[di])
        def _():
            for dj in (-1, 0, 1):
                pl.semaphore_signal(
                    barrier, inc=1, device_id=at(di, dj), device_id_type=MESH
                )

    live_count = count[0, 0]
    part1[...] = jnp.full((8, 128), live_count, jnp.int32).astype(jnp.float32)
    arrivals = sum(len(group) for group in groups)
    for di in (-1, 1):
        arrivals = arrivals + jnp.where(inside[di], 3, 0)
    pl.semaphore_wait(barrier, arrivals)

    def start_phase(phase):
        part, got, sent, received = phases[phase]
        copies = []
        for k, partner in enumerate(groups[phase]):
            copy = pltpu.make_async_remote_copy(
                src_ref=part,
                dst_ref=got.at[k],
                send_sem=sent.at[k],
                recv_sem=received.at[k],
                device_id=partner,
                device_id_type=MESH,
            )
            copy.start()
            copies.append(copy)
        return copies

    def end_phase(phase, copies, result):
        part, got, _, _ = phases[phase]
        for copy in copies:
            copy.wait()
        value = part[...]
        for k in range(len(copies)):
            value = value + got[k]
        result[...] = value

    phases = [
        (part1, got1, send1, recv1),
        (part2, got2, send2, recv2),
        (part3, got3, send3, recv3),
    ]
    counting = start_phase(0)

    for copy in inputs:
        copy.wait()
    fill_scales(scales, diag, shear)
    for r in range(ROWS):
        for k in range(2):
            places[k, r : r + 1, :] = cells[k : k + 1, 128 * r : 128 * r + 128]
    lane = lax.broadcasted_iota(jnp.int32, (8, 128), 1)
    row = lax.broadcasted_iota(jnp.int32, (8, 128), 0)
    keys = [[], [], []]
    for half in range(2):
        rows = slice(8 * half, 8 * half + 8)
        wall = places[0, rows, :] & (TY - 1)
        span = places[1, rows, :] & (TZ - 1)
        key = wall * 2048 + span * 8
        for c in range(3):
            key = key + lax.shift_right_logical(signs[c, rows, :] + 1, 1) * (1 << c)
        live = row * 128 + lane + 1024 * half < live_count
        key = jnp.where(live, key, DEAD)
        keys[0].append(key)
        keys[1].append(jnp.where(span < HALF - 1, key, DEAD))
        keys[2].append(jnp.where(span > HALF, key, DEAD))
    for kind, halves in enumerate(sort_keys([tuple(k) for k in keys])):
        for half, key in enumerate(halves):
            rows = slice(8 * half, 8 * half + 8)
            stage[kind, 0, rows, :] = lax.shift_right_logical(key, 11)
            stage[kind, 1, rows, :] = lax.shift_right_logical(key, 3) & 255
            live = key < DEAD
            for c in range(3):
                sign = (lax.shift_right_logical(key, c) & 1) * 2 - 1
                stage[kind, 2 + c, rows, :] = jnp.where(live, sign, 0)

    sends = {}
    for slot, (di, dj) in enumerate(OFFSETS):
        if slot == OWN:
            continue
        sends[slot] = pltpu.make_async_remote_copy(
            src_ref=stage.at[{0: 0, 1: 1, -1: 2}[dj]],
            dst_ref=arrived.at[slot],
            send_sem=send_sem.at[slot],
            recv_sem=recv_sem.at[slot],
            device_id=at(-di, -dj),
            device_id_type=MESH,
        )
    for dj in (-1, 1):
        sends[4 + dj].start()
    for di in (-1, 1):

        @pl.when(inside[-di])
        def _():
            for dj in (-1, 0, 1):
                sends[4 + 3 * di + dj].start()

    lane16 = lax.broadcasted_iota(jnp.int32, (ROWS, 128), 1)

    def edges(slot, table):
        di, _ = OFFSETS[slot]
        wall = table[0]
        starts = jnp.broadcast_to(wall[:, 0:1], (ROWS, 128))
        ends = jnp.broadcast_to(wall[:, 127:128], (ROWS, 128))
        low = lane16 * BLOCK - (HALF - 1) - TY * di
        high = jnp.minimum(
            (lane16 - BLOCKS) * BLOCK + (BLOCK + HALF - 2) - TY * di, TY - 1
        )
        before = jnp.where(ends < low, 1, 0)
        begun = jnp.where(starts <= high, 1, 0)
        return jnp.sum(jnp.where(lane16 < BLOCKS, before, begun), axis=0, keepdims=True)

    own_edges[...] = jnp.broadcast_to(edges(OWN, stage.at[0]), (8, 128))
    lists[OWN] = stage[0]
    to_scalars = pltpu.make_async_copy(own_edges, own_bounds, bound_sem.at[0])
    to_scalars.start()
    end_phase(0, counting, part2)
    counting = start_phase(1)
    to_scalars.wait()

    def own_block(b):
        begin = own_bounds[0, b]
        number = jnp.maximum(own_bounds[0, BLOCKS + b] - begin, 0)
        own[b] = product(lists, 0, b, [0, begin, 0], [0, number, 0], 0, OWN_CHUNKS)

    pl.loop(0, SPLIT, unroll=UNROLL_OWN)(own_block)
    end_phase(1, counting, part3)
    counting = start_phase(2)

    bounds[OWN : OWN + 1, :] = own_edges[0:1, :]

    def finish(slot):
        lists[slot] = arrived[slot]
        bounds[slot : slot + 1, :] = edges(slot, arrived.at[slot])

    for dj in (-1, 1):
        sends[4 + dj].wait()
        finish(4 + dj)
    for di in (-1, 1):

        @pl.when(inside[-di])
        def _():
            for dj in (-1, 0, 1):
                sends[4 + 3 * di + dj].wait_send()

        @pl.when(inside[di])
        def _():
            for dj in (-1, 0, 1):
                slot = 4 + 3 * di + dj
                sends[slot].wait_recv()
                finish(slot)

        @pl.when(jnp.logical_not(inside[di]))
        def _():
            for dj in (-1, 0, 1):
                slot = 4 + 3 * di + dj
                lists[slot] = jnp.zeros((5, ROWS, 128), jnp.int32)
                bounds[slot : slot + 1, :] = jnp.zeros((1, 128), jnp.int32)

    bounds[9:16, :] = jnp.zeros((7, 128), jnp.int32)
    to_scalars = pltpu.make_async_copy(bounds, list_bounds, bound_sem.at[1])
    to_scalars.start()
    to_scalars.wait()

    def side_block(b):
        parts = {
            dj: product(lists, dj, b, *chunk_counts(list_bounds, dj, b), 0, SIDE_CHUNKS)
            for dj in (-1, 1)
        }
        k = stress(scales, b)
        raw = [
            jnp.concatenate(
                [
                    own[b, :, c * TZ + half * HALF : c * TZ + (half + 1) * HALF]
                    + parts[dj][:, c * HALF : (c + 1) * HALF]
                    for half, dj in ((0, -1), (1, 1))
                ],
                axis=1,
            )
            for c in range(3)
        ]
        for c, value in enumerate(transformed(k, raw)):
            own[b, :, c * TZ : (c + 1) * TZ] = value

    for b in (0, BLOCKS - 1):
        ranges = chunk_counts(list_bounds, 0, b)
        own[b] += product(lists, 0, jnp.int32(b), *ranges, 0, END_CHUNKS)
    pl.loop(0, BLOCKS, unroll=UNROLL_SIDE)(side_block)
    end_phase(2, counting, total)
    fetch.wait()


def fill_scales(scales, diag, shear):
    scales[0:3, :] = diag[...] * (1.5 / (HALF * HALF))
    scales[3:6, :] = shear[...] * (1.5 / (HALF * HALF))
    scales[6:8, :] = jnp.zeros((2, TY), jnp.float32)


def stress(scales, b):
    return scales[:, pl.ds(pl.multiple_of(b * BLOCK, BLOCK), BLOCK)].T


def transformed(k, raw):
    return (
        k[:, 0:1] * raw[0],
        k[:, 3:4] * raw[0] + k[:, 1:2] * raw[1],
        k[:, 4:5] * raw[0] + k[:, 5:6] * raw[1] + k[:, 2:3] * raw[2],
    )


def chunk_counts(bounds, dj, b):
    slots = [(di + 1) * 3 + dj + 1 for di in (-1, 0, 1)]
    begins = [bounds[slot, b] for slot in slots]
    numbers = [
        jnp.maximum(bounds[slot, BLOCKS + b] - begin, 0) for slot, begin in zip(slots, begins)
    ]
    if dj == 0:
        begins[1] = numbers[1] = 0
    return begins, numbers


def product(lists, dj, b, begins, numbers, start, chunks):
    bf = jnp.bfloat16
    left, right = [], []
    above = numbers[0]
    beside = above + numbers[1]
    every = beside + numbers[2]
    for part in range(chunks):
        i = start + part
        di = jnp.where(i < above, 0, jnp.where(i < beside, 1, 2))
        base = jnp.where(
            i < above,
            begins[0],
            jnp.where(i < beside, begins[1] - above, begins[2] - beside),
        )
        used = i < every
        slot = jnp.where(used, di * 3 + dj + 1, OWN)
        chunk = pl.ds(jnp.where(used, base + i, 0), 1)
        live = jnp.where(used, 1, 0)
        anchor = 128 + b * BLOCK - TY * (di - 1)
        left.append(tent(lists[slot, 0, chunk, :] - anchor, BLOCK, -128))
        q = lists[slot, 1, chunk, :] - 128 + TZ * dj
        if dj == 0:
            shape = tent(q, TZ, -128)
        else:
            shape = tent(q, HALF, -128 if dj < 0 else 0)
        signed = [
            shape * (lists[slot, 2 + c, chunk, :] * live).astype(jnp.float32).astype(bf)
            for c in range(3)
        ]
        right.append(jnp.concatenate(signed, axis=0))
    return lax.dot_general(
        jnp.concatenate(left, axis=1),
        jnp.concatenate(right, axis=1),
        (((1,), (1,)), ((), ())),
        preferred_element_type=jnp.float32,
    )


def tent(place, rows, first):
    bf = jnp.bfloat16
    y = (lax.broadcasted_iota(jnp.int32, (rows, 128), 0) + first).astype(jnp.float32).astype(bf)
    near = jnp.minimum(jnp.maximum(place, -256), 256).astype(jnp.float32).astype(bf)
    return jnp.maximum(bf(HALF) - jnp.abs(y - near), bf(0))


def evaluate(bounds, total, lists, diag, shear, own, mean, out, buffer, acc, scales, out_sem):
    def save(b):
        rows = pl.ds(pl.multiple_of(b * BLOCK, BLOCK), BLOCK)
        return pltpu.make_async_copy(buffer.at[:, rows, :], out.at[:, rows, :], out_sem.at[b])

    gain = jnp.sqrt(TY * GY * (TZ * GZ) / (HALF * HALF) / total[0:1, 0:1])

    def finish(b, field):
        rows = pl.ds(pl.multiple_of(b * BLOCK, BLOCK), BLOCK)
        for c in range(3):
            buffer[c, rows, :] = mean[c, rows, :] + gain * field[:, c * TZ : (c + 1) * TZ]
        save(b).start()

    def leftovers(b):
        begin = bounds[OWN, b]
        number = jnp.maximum(bounds[OWN, BLOCKS + b] - begin, 0)
        jobs = [(0, [0, begin, 0], [0, number, 0], OWN_CHUNKS)]
        for dj, done in ((-1, SIDE_CHUNKS), (0, END_CHUNKS), (1, SIDE_CHUNKS)):
            jobs.append((dj, *chunk_counts(bounds, dj, b), done))
        return jobs

    @pl.loop(0, BLOCKS)
    def _(b):
        jobs = leftovers(b)
        counts = [numbers[0] + numbers[1] + numbers[2] for _, _, numbers, _ in jobs]
        some = counts[0] > jobs[0][3]
        for count, job in zip(counts[1:], jobs[1:]):
            some = jnp.logical_or(some, count > job[3])

        @pl.when(some)
        def _():
            acc[...] = jnp.zeros_like(acc)
            for count, (dj, begins, numbers, done) in zip(counts, jobs):

                def more(step, carry, dj=dj, begins=begins, numbers=numbers, done=done):
                    extra = product(lists, dj, b, begins, numbers, done + step * 2, 2)
                    if dj == 0:
                        acc[...] += extra
                    else:
                        for c in range(3):
                            at = c * TZ + (0 if dj < 0 else HALF)
                            acc[:, at : at + HALF] += extra[:, c * HALF : (c + 1) * HALF]
                    return carry

                lax.fori_loop(0, jnp.maximum(count - done + 1, 0) // 2, more, 0)
            fill_scales(scales, diag, shear)
            raw = [acc[:, c * TZ : (c + 1) * TZ] for c in range(3)]
            for c, value in enumerate(transformed(stress(scales, b), raw)):
                acc[:, c * TZ : (c + 1) * TZ] = own[b, :, c * TZ : (c + 1) * TZ] + value
            finish(b, acc)

        @pl.when(jnp.logical_not(some))
        def _():
            finish(b, own.at[b])

    for b in range(BLOCKS):
        save(b).wait()


def body(eddy_cells, eddy_signs, eddy_counts, stress_diag, stress_shear, mean_flow):
    vmem = pl.BlockSpec(memory_space=pltpu.VMEM)
    smem = pl.BlockSpec(memory_space=pltpu.SMEM)
    anywhere = pl.BlockSpec(memory_space=pl.ANY)
    hbm = pl.BlockSpec(memory_space=pltpu.HBM)
    dma = pltpu.SemaphoreType.DMA
    f32, i32 = jnp.float32, jnp.int32
    lists, bounds, total, own, held = pl.pallas_call(
        exchange,
        out_shape=(
            pltpu.VMEM((9, 5, ROWS, 128), i32),
            jax.ShapeDtypeStruct((16, 128), jnp.int32),
            pltpu.VMEM((8, 128), f32),
            pltpu.VMEM((BLOCKS, BLOCK, 3 * TZ), f32),
            pltpu.VMEM((3, TY, TZ), f32),
        ),
        in_specs=[hbm, hbm, smem, hbm, hbm, hbm],
        out_specs=(vmem, vmem, vmem, vmem, vmem),
        scratch_shapes=[
            pltpu.VMEM((2, ROWS, 128), jnp.int32),
            pltpu.VMEM((3, 5, ROWS, 128), i32),
            pltpu.VMEM((8, 128), i32),
            pltpu.SMEM((8, 128), i32),
            pltpu.SMEM((16, 128), i32),
            dma((2,)),
            pltpu.VMEM((9, 5, ROWS, 128), i32),
            pltpu.VMEM((8, 128), f32),
            pltpu.VMEM((GZ - 1, 8, 128), f32),
            pltpu.VMEM((8, 128), f32),
            pltpu.VMEM((3, 8, 128), f32),
            dma((9,)),
            dma((9,)),
            dma((GZ - 1,)),
            dma((GZ - 1,)),
            dma((3,)),
            dma((3,)),
            pltpu.VMEM((8, 128), f32),
            pltpu.VMEM((3, 8, 128), f32),
            dma((3,)),
            dma((3,)),
            dma,
            pltpu.VMEM((2, CAP), jnp.int32),
            pltpu.VMEM((3, ROWS, 128), jnp.int32),
            dma((4,)),
            pltpu.VMEM((8, TY), f32),
            pltpu.VMEM((3, TY), f32),
            pltpu.VMEM((3, TY), f32),
        ],
        compiler_params=pltpu.CompilerParams(
            collective_id=0, has_side_effects=True, vmem_limit_bytes=VMEM_LIMIT
        ),
        name="exchange",
    )(
        pltpu.with_memory_space_constraint(eddy_cells.reshape(2, CAP), pltpu.HBM),
        pltpu.with_memory_space_constraint(eddy_signs.reshape(3, ROWS, 128), pltpu.HBM),
        eddy_counts,
        pltpu.with_memory_space_constraint(stress_diag, pltpu.HBM),
        pltpu.with_memory_space_constraint(stress_shear, pltpu.HBM),
        mean_flow,
    )
    return pl.pallas_call(
        evaluate,
        out_shape=jax.ShapeDtypeStruct((3, TY, TZ), f32),
        in_specs=[smem, vmem, vmem, vmem, vmem, vmem, vmem],
        out_specs=anywhere,
        scratch_shapes=[
            pltpu.VMEM((3, TY, TZ), f32),
            pltpu.VMEM((BLOCK, 3 * TZ), f32),
            pltpu.VMEM((8, TY), f32),
            dma((BLOCKS,)),
        ],
        compiler_params=pltpu.CompilerParams(vmem_limit_bytes=VMEM_LIMIT),
        name="evaluate",
    )(bounds, total, lists, stress_diag, stress_shear, own, held)


def solution(mesh):
    return jax.shard_map(
        body,
        mesh=mesh,
        in_specs=(
            P("gy", "gz", None, None),
            P("gy", "gz", None, None),
            P("gy", "gz"),
            P(None, "gy"),
            P(None, "gy"),
            P(None, "gy", "gz"),
        ),
        out_specs=P(None, "gy", "gz"),
        check_vma=False,
    )
```

```python
import jax
import jax.numpy as jnp
from jax import lax
from jax.experimental import pallas as pl
from jax.experimental.pallas import tpu as pltpu
from jax.sharding import PartitionSpec as P

TY = 2048
TZ = 256
CAP = 2048
HALF = 128
GY = 16
GZ = 8
ROWS = CAP // 128
BLOCK = 256
BLOCKS = TY // BLOCK
DEAD = 1 << 22
VMEM_LIMIT = 36 << 20
MESH = pl.DeviceIdType.MESH
OFFSETS = tuple((di, dj) for di in (-1, 0, 1) for dj in (-1, 0, 1))
OWN = 4
SPLIT = 8
UNROLL_OWN = 2
UNROLL_SIDE = 2
OWN_CHUNKS = 6
SIDE_CHUNKS = 4
END_CHUNKS = 2


def sort_keys(vregs):
    lane = lax.broadcasted_iota(jnp.int32, (8, 128), 1)
    row = lax.broadcasted_iota(jnp.int32, (8, 128), 0)
    flat = [half for halves in vregs for half in halves]
    flat += [jnp.zeros((8, 128), jnp.int32)] * (16 - len(flat))
    turned = jnp.concatenate(flat, axis=0).T
    x = [turned[8 * i : 8 * i + 8, :] for i in range(16)]
    zero = {t: (lax.shift_right_logical(row, t) & 1) == 0 for t in range(3)}
    zero |= {t: (lax.shift_right_logical(lane, t - 7) & 1) == 0 for t in range(7, 11)}

    def rising(up, i):
        if up == 11:
            return True
        if 3 <= up < 7:
            return not (i >> (up - 3)) & 1
        return zero[up]

    for up in range(1, 12):
        for step in range(up - 1, -1, -1):
            new = [None] * 16
            if 3 <= step < 7:
                for i in range(16):
                    j = i ^ (1 << (step - 3))
                    if j < i:
                        continue
                    low, high = jnp.minimum(x[i], x[j]), jnp.maximum(x[i], x[j])
                    r = rising(up, i)
                    if r is True:
                        new[i], new[j] = low, high
                    elif r is False:
                        new[i], new[j] = high, low
                    else:
                        new[i], new[j] = jnp.where(r, low, high), jnp.where(r, high, low)
            else:
                axis, size, by = (0, 8, 1 << step) if step < 3 else (1, 128, 1 << (step - 7))
                lower = zero[step]
                same = None
                for i in range(16):
                    ahead = pltpu.roll(x[i], size - by, axis)
                    if 2 * by == size:
                        other = ahead
                    else:
                        other = jnp.where(lower, ahead, pltpu.roll(x[i], by, axis))
                    low, high = jnp.minimum(x[i], other), jnp.maximum(x[i], other)
                    r = rising(up, i)
                    if r is True:
                        new[i] = jnp.where(lower, low, high)
                    elif r is False:
                        new[i] = jnp.where(lower, high, low)
                    else:
                        same = lower == r if same is None else same
                        new[i] = jnp.where(same, low, high)
            x = new
    back = jnp.concatenate(x, axis=0).T
    return [(back[16 * i : 16 * i + 8, :], back[16 * i + 8 : 16 * i + 16, :]) for i in range(len(vregs))]


def exchange(
    cells_in,
    signs_in,
    count,
    diag_in,
    shear_in,
    mean,
    lists,
    bounds,
    total,
    own,
    held,
    places,
    stage,
    own_edges,
    own_bounds,
    list_bounds,
    bound_sem,
    arrived,
    part1,
    got1,
    part2,
    got2,
    send_sem,
    recv_sem,
    send1,
    recv1,
    send2,
    recv2,
    part3,
    got3,
    send3,
    recv3,
    mean_sem,
    cells,
    signs,
    input_sem,
    scales,
    diag,
    shear,
):
    inputs = [
        pltpu.make_async_copy(cells_in, cells, input_sem.at[0]),
        pltpu.make_async_copy(signs_in, signs, input_sem.at[1]),
        pltpu.make_async_copy(diag_in, diag, input_sem.at[2]),
        pltpu.make_async_copy(shear_in, shear, input_sem.at[3]),
    ]
    for copy in inputs:
        copy.start()
    fetch = pltpu.make_async_copy(mean, held, mean_sem)
    fetch.start()
    gy = lax.axis_index("gy")
    gz = lax.axis_index("gz")
    barrier = pltpu.get_barrier_semaphore()

    def at(di, dj):
        return (lax.rem(gy + di + GY, GY), lax.rem(gz + dj + GZ, GZ))

    def along_y(d):
        return (gy - lax.rem(gy, 4) + lax.rem(gy + d, 4), gz)

    groups = [
        [at(4 * d, 0) for d in range(1, 4)],
        [along_y(d) for d in range(1, 4)],
        [at(0, d) for d in range(1, GZ)],
    ]
    for group in groups:
        for partner in group:
            pl.semaphore_signal(barrier, inc=1, device_id=partner, device_id_type=MESH)
    inside = {di: jnp.logical_and(gy + di >= 0, gy + di < GY) for di in (-1, 1)}
    for di in (-1, 1):

        @pl.when(inside[di])
        def _():
            for dj in (-1, 0, 1):
                pl.semaphore_signal(
                    barrier, inc=1, device_id=at(di, dj), device_id_type=MESH
                )

    live_count = count[0, 0]
    part1[...] = jnp.full((8, 128), live_count, jnp.int32).astype(jnp.float32)
    arrivals = sum(len(group) for group in groups)
    for di in (-1, 1):
        arrivals = arrivals + jnp.where(inside[di], 3, 0)
    pl.semaphore_wait(barrier, arrivals)

    def start_phase(phase):
        part, got, sent, received = phases[phase]
        copies = []
        for k, partner in enumerate(groups[phase]):
            copy = pltpu.make_async_remote_copy(
                src_ref=part,
                dst_ref=got.at[k],
                send_sem=sent.at[k],
                recv_sem=received.at[k],
                device_id=partner,
                device_id_type=MESH,
            )
            copy.start()
            copies.append(copy)
        return copies

    def end_phase(phase, copies, result):
        part, got, _, _ = phases[phase]
        for copy in copies:
            copy.wait()
        value = part[...]
        for k in range(len(copies)):
            value = value + got[k]
        result[...] = value

    phases = [
        (part1, got1, send1, recv1),
        (part2, got2, send2, recv2),
        (part3, got3, send3, recv3),
    ]
    counting = start_phase(0)

    for copy in inputs:
        copy.wait()
    fill_scales(scales, diag, shear)
    for r in range(ROWS):
        for k in range(2):
            places[k, r : r + 1, :] = cells[k : k + 1, 128 * r : 128 * r + 128]
    lane = lax.broadcasted_iota(jnp.int32, (8, 128), 1)
    row = lax.broadcasted_iota(jnp.int32, (8, 128), 0)
    keys = [[], [], []]
    for half in range(2):
        rows = slice(8 * half, 8 * half + 8)
        wall = places[0, rows, :] & (TY - 1)
        span = places[1, rows, :] & (TZ - 1)
        key = wall * 2048 + span * 8
        for c in range(3):
            key = key + lax.shift_right_logical(signs[c, rows, :] + 1, 1) * (1 << c)
        live = row * 128 + lane + 1024 * half < live_count
        key = jnp.where(live, key, DEAD)
        keys[0].append(key)
        keys[1].append(jnp.where(span < HALF - 1, key, DEAD))
        keys[2].append(jnp.where(span > HALF, key, DEAD))
    for kind, halves in enumerate(sort_keys([tuple(k) for k in keys])):
        for half, key in enumerate(halves):
            rows = slice(8 * half, 8 * half + 8)
            stage[kind, 0, rows, :] = lax.shift_right_logical(key, 11)
            stage[kind, 1, rows, :] = lax.shift_right_logical(key, 3) & 255
            live = key < DEAD
            for c in range(3):
                sign = (lax.shift_right_logical(key, c) & 1) * 2 - 1
                stage[kind, 2 + c, rows, :] = jnp.where(live, sign, 0)

    sends = {}
    for slot, (di, dj) in enumerate(OFFSETS):
        if slot == OWN:
            continue
        sends[slot] = pltpu.make_async_remote_copy(
            src_ref=stage.at[{0: 0, 1: 1, -1: 2}[dj]],
            dst_ref=arrived.at[slot],
            send_sem=send_sem.at[slot],
            recv_sem=recv_sem.at[slot],
            device_id=at(-di, -dj),
            device_id_type=MESH,
        )
    for dj in (-1, 1):
        sends[4 + dj].start()
    for di in (-1, 1):

        @pl.when(inside[-di])
        def _():
            for dj in (-1, 0, 1):
                sends[4 + 3 * di + dj].start()

    lane16 = lax.broadcasted_iota(jnp.int32, (ROWS, 128), 1)

    def edges(slot, table):
        di, _ = OFFSETS[slot]
        wall = table[0]
        starts = jnp.broadcast_to(wall[:, 0:1], (ROWS, 128))
        ends = jnp.broadcast_to(wall[:, 127:128], (ROWS, 128))
        low = lane16 * BLOCK - (HALF - 1) - TY * di
        high = jnp.minimum(
            (lane16 - BLOCKS) * BLOCK + (BLOCK + HALF - 2) - TY * di, TY - 1
        )
        before = jnp.where(ends < low, 1, 0)
        begun = jnp.where(starts <= high, 1, 0)
        return jnp.sum(jnp.where(lane16 < BLOCKS, before, begun), axis=0, keepdims=True)

    own_edges[...] = jnp.broadcast_to(edges(OWN, stage.at[0]), (8, 128))
    lists[OWN] = stage[0]
    to_scalars = pltpu.make_async_copy(own_edges, own_bounds, bound_sem.at[0])
    to_scalars.start()
    to_scalars.wait()

    def own_block(b):
        begin = own_bounds[0, b]
        number = jnp.maximum(own_bounds[0, BLOCKS + b] - begin, 0)
        own[b] = product(lists, 0, b, [0, begin, 0], [0, number, 0], 0, OWN_CHUNKS)

    pl.loop(0, 2, unroll=UNROLL_OWN)(own_block)
    end_phase(0, counting, part2)
    counting = start_phase(1)
    pl.loop(2, 8, unroll=UNROLL_OWN)(own_block)
    end_phase(1, counting, part3)
    counting = start_phase(2)

    bounds[OWN : OWN + 1, :] = own_edges[0:1, :]

    def finish(slot):
        lists[slot] = arrived[slot]
        bounds[slot : slot + 1, :] = edges(slot, arrived.at[slot])

    for dj in (-1, 1):
        sends[4 + dj].wait()
        finish(4 + dj)
    for di in (-1, 1):

        @pl.when(inside[-di])
        def _():
            for dj in (-1, 0, 1):
                sends[4 + 3 * di + dj].wait_send()

        @pl.when(inside[di])
        def _():
            for dj in (-1, 0, 1):
                slot = 4 + 3 * di + dj
                sends[slot].wait_recv()
                finish(slot)

        @pl.when(jnp.logical_not(inside[di]))
        def _():
            for dj in (-1, 0, 1):
                slot = 4 + 3 * di + dj
                lists[slot] = jnp.zeros((5, ROWS, 128), jnp.int32)
                bounds[slot : slot + 1, :] = jnp.zeros((1, 128), jnp.int32)

    every = [bounds[slot : slot + 1, :] for slot in range(9)]
    number = [jnp.maximum(pltpu.roll(row, 128 - BLOCKS, 1) - row, 0) for row in every]
    over = [
        number[OWN] - OWN_CHUNKS,
        number[1] + number[7] - END_CHUNKS,
        number[0] + number[3] + number[6] - SIDE_CHUNKS,
        number[2] + number[5] + number[8] - SIDE_CHUNKS,
    ]
    most = jnp.maximum(jnp.maximum(over[0], over[1]), jnp.maximum(over[2], over[3]))
    most = jnp.max(jnp.where(lane16[0:1, :] < BLOCKS, most, 0), axis=1, keepdims=True)
    bounds[9:16, :] = jnp.broadcast_to(most, (7, 128))
    to_scalars = pltpu.make_async_copy(bounds, list_bounds, bound_sem.at[1])
    to_scalars.start()
    to_scalars.wait()

    def side_block(b):
        parts = {
            dj: product(lists, dj, b, *chunk_counts(list_bounds, dj, b), 0, SIDE_CHUNKS)
            for dj in (-1, 1)
        }
        k = stress(scales, b)
        raw = [
            jnp.concatenate(
                [
                    own[b, :, c * TZ + half * HALF : c * TZ + (half + 1) * HALF]
                    + parts[dj][:, c * HALF : (c + 1) * HALF]
                    for half, dj in ((0, -1), (1, 1))
                ],
                axis=1,
            )
            for c in range(3)
        ]
        for c, value in enumerate(transformed(k, raw)):
            own[b, :, c * TZ : (c + 1) * TZ] = value

    for b in (0, BLOCKS - 1):
        ranges = chunk_counts(list_bounds, 0, b)
        own[b] += product(lists, 0, jnp.int32(b), *ranges, 0, END_CHUNKS)
    pl.loop(0, BLOCKS, unroll=UNROLL_SIDE)(side_block)
    end_phase(2, counting, total)
    fetch.wait()


def fill_scales(scales, diag, shear):
    scales[0:3, :] = diag[...] * (1.5 / (HALF * HALF))
    scales[3:6, :] = shear[...] * (1.5 / (HALF * HALF))
    scales[6:8, :] = jnp.zeros((2, TY), jnp.float32)


def stress(scales, b):
    return scales[:, pl.ds(pl.multiple_of(b * BLOCK, BLOCK), BLOCK)].T


def transformed(k, raw):
    return (
        k[:, 0:1] * raw[0],
        k[:, 3:4] * raw[0] + k[:, 1:2] * raw[1],
        k[:, 4:5] * raw[0] + k[:, 5:6] * raw[1] + k[:, 2:3] * raw[2],
    )


def chunk_counts(bounds, dj, b):
    slots = [(di + 1) * 3 + dj + 1 for di in (-1, 0, 1)]
    begins = [bounds[slot, b] for slot in slots]
    numbers = [
        jnp.maximum(bounds[slot, BLOCKS + b] - begin, 0) for slot, begin in zip(slots, begins)
    ]
    if dj == 0:
        begins[1] = numbers[1] = 0
    return begins, numbers


def product(lists, dj, b, begins, numbers, start, chunks):
    bf = jnp.bfloat16
    left, right = [], []
    above = numbers[0]
    beside = above + numbers[1]
    every = beside + numbers[2]
    for part in range(chunks):
        i = start + part
        di = jnp.where(i < above, 0, jnp.where(i < beside, 1, 2))
        base = jnp.where(
            i < above,
            begins[0],
            jnp.where(i < beside, begins[1] - above, begins[2] - beside),
        )
        used = i < every
        slot = jnp.where(used, di * 3 + dj + 1, OWN)
        chunk = pl.ds(jnp.where(used, base + i, 0), 1)
        live = jnp.where(used, 1, 0)
        anchor = 128 + b * BLOCK - TY * (di - 1)
        left.append(tent(lists[slot, 0, chunk, :] - anchor, BLOCK, -128))
        q = lists[slot, 1, chunk, :] - 128 + TZ * dj
        if dj == 0:
            shape = tent(q, TZ, -128)
        else:
            shape = tent(q, HALF, -128 if dj < 0 else 0)
        signed = [
            shape * (lists[slot, 2 + c, chunk, :] * live).astype(jnp.float32).astype(bf)
            for c in range(3)
        ]
        right.append(jnp.concatenate(signed, axis=0))
    return lax.dot_general(
        jnp.concatenate(left, axis=1),
        jnp.concatenate(right, axis=1),
        (((1,), (1,)), ((), ())),
        preferred_element_type=jnp.float32,
    )


def tent(place, rows, first):
    bf = jnp.bfloat16
    y = (lax.broadcasted_iota(jnp.int32, (rows, 128), 0) + first).astype(jnp.float32).astype(bf)
    near = jnp.minimum(jnp.maximum(place, -256), 256).astype(jnp.float32).astype(bf)
    return jnp.maximum(bf(HALF) - jnp.abs(y - near), bf(0))


def evaluate(bounds, total, lists, diag, shear, own, mean, out, buffer, acc, scales, out_sem):
    def save(b):
        rows = pl.ds(pl.multiple_of(b * BLOCK, BLOCK), BLOCK)
        return pltpu.make_async_copy(buffer.at[:, rows, :], out.at[:, rows, :], out_sem.at[b])

    gain = jnp.sqrt(TY * GY * (TZ * GZ) / (HALF * HALF) / total[0:1, 0:1])

    def finish(b, field):
        rows = pl.ds(pl.multiple_of(b * BLOCK, BLOCK), BLOCK)
        for c in range(3):
            buffer[c, rows, :] = mean[c, rows, :] + gain * field[:, c * TZ : (c + 1) * TZ]
        save(b).start()

    def leftovers(b):
        begin = bounds[OWN, b]
        number = jnp.maximum(bounds[OWN, BLOCKS + b] - begin, 0)
        jobs = [(0, [0, begin, 0], [0, number, 0], OWN_CHUNKS)]
        for dj, done in ((-1, SIDE_CHUNKS), (0, END_CHUNKS), (1, SIDE_CHUNKS)):
            jobs.append((dj, *chunk_counts(bounds, dj, b), done))
        return jobs

    leftover = bounds[9, 0]

    @pl.when(leftover == 0)
    def _():
        for b in range(BLOCKS):
            finish(b, own.at[b])

    @pl.when(leftover > 0)
    def _():
        @pl.loop(0, BLOCKS)
        def _(b):
            jobs = leftovers(b)
            counts = [numbers[0] + numbers[1] + numbers[2] for _, _, numbers, _ in jobs]
            some = counts[0] > jobs[0][3]
            for count, job in zip(counts[1:], jobs[1:]):
                some = jnp.logical_or(some, count > job[3])

            @pl.when(some)
            def _():
                acc[...] = jnp.zeros_like(acc)
                for count, (dj, begins, numbers, done) in zip(counts, jobs):

                    def more(step, carry, dj=dj, begins=begins, numbers=numbers, done=done):
                        extra = product(lists, dj, b, begins, numbers, done + step * 2, 2)
                        if dj == 0:
                            acc[...] += extra
                        else:
                            for c in range(3):
                                at = c * TZ + (0 if dj < 0 else HALF)
                                acc[:, at : at + HALF] += extra[:, c * HALF : (c + 1) * HALF]
                        return carry

                    lax.fori_loop(0, jnp.maximum(count - done + 1, 0) // 2, more, 0)
                fill_scales(scales, diag, shear)
                raw = [acc[:, c * TZ : (c + 1) * TZ] for c in range(3)]
                for c, value in enumerate(transformed(stress(scales, b), raw)):
                    acc[:, c * TZ : (c + 1) * TZ] = own[b, :, c * TZ : (c + 1) * TZ] + value
                finish(b, acc)

            @pl.when(jnp.logical_not(some))
            def _():
                finish(b, own.at[b])

    for b in range(BLOCKS):
        save(b).wait()


def body(eddy_cells, eddy_signs, eddy_counts, stress_diag, stress_shear, mean_flow):
    vmem = pl.BlockSpec(memory_space=pltpu.VMEM)
    smem = pl.BlockSpec(memory_space=pltpu.SMEM)
    anywhere = pl.BlockSpec(memory_space=pl.ANY)
    hbm = pl.BlockSpec(memory_space=pltpu.HBM)
    dma = pltpu.SemaphoreType.DMA
    f32, i32 = jnp.float32, jnp.int32
    lists, bounds, total, own, held = pl.pallas_call(
        exchange,
        out_shape=(
            pltpu.VMEM((9, 5, ROWS, 128), i32),
            jax.ShapeDtypeStruct((16, 128), jnp.int32),
            pltpu.VMEM((8, 128), f32),
            pltpu.VMEM((BLOCKS, BLOCK, 3 * TZ), f32),
            pltpu.VMEM((3, TY, TZ), f32),
        ),
        in_specs=[hbm, hbm, smem, hbm, hbm, hbm],
        out_specs=(vmem, vmem, vmem, vmem, vmem),
        scratch_shapes=[
            pltpu.VMEM((2, ROWS, 128), jnp.int32),
            pltpu.VMEM((3, 5, ROWS, 128), i32),
            pltpu.VMEM((8, 128), i32),
            pltpu.SMEM((8, 128), i32),
            pltpu.SMEM((16, 128), i32),
            dma((2,)),
            pltpu.VMEM((9, 5, ROWS, 128), i32),
            pltpu.VMEM((8, 128), f32),
            pltpu.VMEM((3, 8, 128), f32),
            pltpu.VMEM((8, 128), f32),
            pltpu.VMEM((3, 8, 128), f32),
            dma((9,)),
            dma((9,)),
            dma((3,)),
            dma((3,)),
            dma((3,)),
            dma((3,)),
            pltpu.VMEM((8, 128), f32),
            pltpu.VMEM((GZ - 1, 8, 128), f32),
            dma((GZ - 1,)),
            dma((GZ - 1,)),
            dma,
            pltpu.VMEM((2, CAP), jnp.int32),
            pltpu.VMEM((3, ROWS, 128), jnp.int32),
            dma((4,)),
            pltpu.VMEM((8, TY), f32),
            pltpu.VMEM((3, TY), f32),
            pltpu.VMEM((3, TY), f32),
        ],
        compiler_params=pltpu.CompilerParams(
            collective_id=0, has_side_effects=True, vmem_limit_bytes=VMEM_LIMIT
        ),
        name="exchange",
    )(
        pltpu.with_memory_space_constraint(eddy_cells.reshape(2, CAP), pltpu.HBM),
        pltpu.with_memory_space_constraint(eddy_signs.reshape(3, ROWS, 128), pltpu.HBM),
        eddy_counts,
        pltpu.with_memory_space_constraint(stress_diag, pltpu.HBM),
        pltpu.with_memory_space_constraint(stress_shear, pltpu.HBM),
        mean_flow,
    )
    return pl.pallas_call(
        evaluate,
        out_shape=jax.ShapeDtypeStruct((3, TY, TZ), f32),
        in_specs=[smem, vmem, vmem, vmem, vmem, vmem, vmem],
        out_specs=anywhere,
        scratch_shapes=[
            pltpu.VMEM((3, TY, TZ), f32),
            pltpu.VMEM((BLOCK, 3 * TZ), f32),
            pltpu.VMEM((8, TY), f32),
            dma((BLOCKS,)),
        ],
        compiler_params=pltpu.CompilerParams(vmem_limit_bytes=VMEM_LIMIT),
        name="evaluate",
    )(bounds, total, lists, stress_diag, stress_shear, own, held)


def solution(mesh):
    return jax.shard_map(
        body,
        mesh=mesh,
        in_specs=(
            P("gy", "gz", None, None),
            P("gy", "gz", None, None),
            P("gy", "gz"),
            P(None, "gy"),
            P(None, "gy"),
            P(None, "gy", "gz"),
        ),
        out_specs=P(None, "gy", "gz"),
        check_vma=False,
    )
```

```python
import jax
import jax.numpy as jnp
from jax import lax
from jax.experimental import pallas as pl
from jax.experimental.pallas import tpu as pltpu
from jax.sharding import PartitionSpec as P

TY = 2048
TZ = 256
CAP = 2048
HALF = 128
GY = 16
GZ = 8
ROWS = CAP // 128
BLOCK = 256
BLOCKS = TY // BLOCK
DEAD = 1 << 22
VMEM_LIMIT = 36 << 20
MESH = pl.DeviceIdType.MESH
OFFSETS = tuple((di, dj) for di in (-1, 0, 1) for dj in (-1, 0, 1))
OWN = 4
SPLIT = 8
UNROLL_OWN = 2
UNROLL_SIDE = 4
OWN_CHUNKS = 6
SIDE_CHUNKS = 4
END_CHUNKS = 2


def sort_keys(vregs):
    lane = lax.broadcasted_iota(jnp.int32, (8, 128), 1)
    row = lax.broadcasted_iota(jnp.int32, (8, 128), 0)
    flat = [half for halves in vregs for half in halves]
    flat += [jnp.zeros((8, 128), jnp.int32)] * (16 - len(flat))
    turned = jnp.concatenate(flat, axis=0).T
    x = [turned[8 * i : 8 * i + 8, :] for i in range(16)]
    zero = {t: (lax.shift_right_logical(row, t) & 1) == 0 for t in range(3)}
    zero |= {t: (lax.shift_right_logical(lane, t - 7) & 1) == 0 for t in range(7, 11)}

    def rising(up, i):
        if up == 11:
            return True
        if 3 <= up < 7:
            return not (i >> (up - 3)) & 1
        return zero[up]

    for up in range(1, 12):
        for step in range(up - 1, -1, -1):
            new = [None] * 16
            if 3 <= step < 7:
                for i in range(16):
                    j = i ^ (1 << (step - 3))
                    if j < i:
                        continue
                    low, high = jnp.minimum(x[i], x[j]), jnp.maximum(x[i], x[j])
                    r = rising(up, i)
                    if r is True:
                        new[i], new[j] = low, high
                    elif r is False:
                        new[i], new[j] = high, low
                    else:
                        new[i], new[j] = jnp.where(r, low, high), jnp.where(r, high, low)
            else:
                axis, size, by = (0, 8, 1 << step) if step < 3 else (1, 128, 1 << (step - 7))
                lower = zero[step]
                same = None
                for i in range(16):
                    ahead = pltpu.roll(x[i], size - by, axis)
                    if 2 * by == size:
                        other = ahead
                    else:
                        other = jnp.where(lower, ahead, pltpu.roll(x[i], by, axis))
                    low, high = jnp.minimum(x[i], other), jnp.maximum(x[i], other)
                    r = rising(up, i)
                    if r is True:
                        new[i] = jnp.where(lower, low, high)
                    elif r is False:
                        new[i] = jnp.where(lower, high, low)
                    else:
                        same = lower == r if same is None else same
                        new[i] = jnp.where(same, low, high)
            x = new
    back = jnp.concatenate(x, axis=0).T
    return [(back[16 * i : 16 * i + 8, :], back[16 * i + 8 : 16 * i + 16, :]) for i in range(len(vregs))]


def exchange(
    cells_in,
    signs_in,
    count,
    diag_in,
    shear_in,
    mean,
    lists,
    bounds,
    total,
    own,
    held,
    places,
    stage,
    own_edges,
    own_bounds,
    list_bounds,
    bound_sem,
    arrived,
    part1,
    got1,
    part2,
    got2,
    send_sem,
    recv_sem,
    send1,
    recv1,
    send2,
    recv2,
    part3,
    got3,
    send3,
    recv3,
    mean_sem,
    cells,
    signs,
    input_sem,
    scales,
    diag,
    shear,
):
    inputs = [
        pltpu.make_async_copy(cells_in, cells, input_sem.at[0]),
        pltpu.make_async_copy(signs_in, signs, input_sem.at[1]),
        pltpu.make_async_copy(diag_in, diag, input_sem.at[2]),
        pltpu.make_async_copy(shear_in, shear, input_sem.at[3]),
    ]
    for copy in inputs:
        copy.start()
    fetch = pltpu.make_async_copy(mean, held, mean_sem)
    fetch.start()
    gy = lax.axis_index("gy")
    gz = lax.axis_index("gz")
    barrier = pltpu.get_barrier_semaphore()

    def at(di, dj):
        return (lax.rem(gy + di + GY, GY), lax.rem(gz + dj + GZ, GZ))

    def along_y(d):
        return (gy - lax.rem(gy, 4) + lax.rem(gy + d, 4), gz)

    groups = [
        [at(4 * d, 0) for d in range(1, 4)],
        [along_y(d) for d in range(1, 4)],
        [at(0, d) for d in range(1, GZ)],
    ]
    for group in groups:
        for partner in group:
            pl.semaphore_signal(barrier, inc=1, device_id=partner, device_id_type=MESH)
    inside = {di: jnp.logical_and(gy + di >= 0, gy + di < GY) for di in (-1, 1)}
    for di in (-1, 1):

        @pl.when(inside[di])
        def _():
            for dj in (-1, 0, 1):
                pl.semaphore_signal(
                    barrier, inc=1, device_id=at(di, dj), device_id_type=MESH
                )

    live_count = count[0, 0]
    part1[...] = jnp.full((8, 128), live_count, jnp.int32).astype(jnp.float32)
    arrivals = sum(len(group) for group in groups)
    for di in (-1, 1):
        arrivals = arrivals + jnp.where(inside[di], 3, 0)
    pl.semaphore_wait(barrier, arrivals)

    def start_phase(phase):
        part, got, sent, received = phases[phase]
        copies = []
        for k, partner in enumerate(groups[phase]):
            copy = pltpu.make_async_remote_copy(
                src_ref=part,
                dst_ref=got.at[k],
                send_sem=sent.at[k],
                recv_sem=received.at[k],
                device_id=partner,
                device_id_type=MESH,
            )
            copy.start()
            copies.append(copy)
        return copies

    def end_phase(phase, copies, result):
        part, got, _, _ = phases[phase]
        for copy in copies:
            copy.wait()
        value = part[...]
        for k in range(len(copies)):
            value = value + got[k]
        result[...] = value

    phases = [
        (part1, got1, send1, recv1),
        (part2, got2, send2, recv2),
        (part3, got3, send3, recv3),
    ]
    counting = start_phase(0)

    for copy in inputs:
        copy.wait()
    fill_scales(scales, diag, shear)
    for r in range(ROWS):
        for k in range(2):
            places[k, r : r + 1, :] = cells[k : k + 1, 128 * r : 128 * r + 128]
    lane = lax.broadcasted_iota(jnp.int32, (8, 128), 1)
    row = lax.broadcasted_iota(jnp.int32, (8, 128), 0)
    keys = [[], [], []]
    for half in range(2):
        rows = slice(8 * half, 8 * half + 8)
        wall = places[0, rows, :] & (TY - 1)
        span = places[1, rows, :] & (TZ - 1)
        key = wall * 2048 + span * 8
        for c in range(3):
            key = key + lax.shift_right_logical(signs[c, rows, :] + 1, 1) * (1 << c)
        live = row * 128 + lane + 1024 * half < live_count
        key = jnp.where(live, key, DEAD)
        keys[0].append(key)
        keys[1].append(jnp.where(span < HALF - 1, key, DEAD))
        keys[2].append(jnp.where(span > HALF, key, DEAD))
    for kind, halves in enumerate(sort_keys([tuple(k) for k in keys])):
        for half, key in enumerate(halves):
            rows = slice(8 * half, 8 * half + 8)
            stage[kind, 0, rows, :] = lax.shift_right_logical(key, 11)
            stage[kind, 1, rows, :] = lax.shift_right_logical(key, 3) & 255
            live = key < DEAD
            for c in range(3):
                sign = (lax.shift_right_logical(key, c) & 1) * 2 - 1
                stage[kind, 2 + c, rows, :] = jnp.where(live, sign, 0)

    sends = {}
    for slot, (di, dj) in enumerate(OFFSETS):
        if slot == OWN:
            continue
        sends[slot] = pltpu.make_async_remote_copy(
            src_ref=stage.at[{0: 0, 1: 1, -1: 2}[dj]],
            dst_ref=arrived.at[slot],
            send_sem=send_sem.at[slot],
            recv_sem=recv_sem.at[slot],
            device_id=at(-di, -dj),
            device_id_type=MESH,
        )
    for dj in (-1, 1):
        sends[4 + dj].start()
    for di in (-1, 1):

        @pl.when(inside[-di])
        def _():
            for dj in (-1, 0, 1):
                sends[4 + 3 * di + dj].start()

    lane16 = lax.broadcasted_iota(jnp.int32, (ROWS, 128), 1)

    def edges(slot, table):
        di, _ = OFFSETS[slot]
        wall = table[0]
        starts = jnp.broadcast_to(wall[:, 0:1], (ROWS, 128))
        ends = jnp.broadcast_to(wall[:, 127:128], (ROWS, 128))
        low = lane16 * BLOCK - (HALF - 1) - TY * di
        high = jnp.minimum(
            (lane16 - BLOCKS) * BLOCK + (BLOCK + HALF - 2) - TY * di, TY - 1
        )
        before = jnp.where(ends < low, 1, 0)
        begun = jnp.where(starts <= high, 1, 0)
        return jnp.sum(jnp.where(lane16 < BLOCKS, before, begun), axis=0, keepdims=True)

    own_edges[...] = jnp.broadcast_to(edges(OWN, stage.at[0]), (8, 128))
    lists[OWN] = stage[0]
    to_scalars = pltpu.make_async_copy(own_edges, own_bounds, bound_sem.at[0])
    to_scalars.start()
    to_scalars.wait()

    def own_block(b):
        begin = own_bounds[0, b]
        number = jnp.maximum(own_bounds[0, BLOCKS + b] - begin, 0)
        own[b] = product(lists, 0, b, [0, begin, 0], [0, number, 0], 0, OWN_CHUNKS)

    pl.loop(0, 2, unroll=UNROLL_OWN)(own_block)
    end_phase(0, counting, part2)
    counting = start_phase(1)
    pl.loop(2, 8, unroll=UNROLL_OWN)(own_block)
    end_phase(1, counting, part3)
    counting = start_phase(2)

    bounds[OWN : OWN + 1, :] = own_edges[0:1, :]

    def finish(slot):
        lists[slot] = arrived[slot]
        bounds[slot : slot + 1, :] = edges(slot, arrived.at[slot])

    for dj in (-1, 1):
        sends[4 + dj].wait()
        finish(4 + dj)
    for di in (-1, 1):

        @pl.when(inside[-di])
        def _():
            for dj in (-1, 0, 1):
                sends[4 + 3 * di + dj].wait_send()

        @pl.when(inside[di])
        def _():
            for dj in (-1, 0, 1):
                slot = 4 + 3 * di + dj
                sends[slot].wait_recv()
                finish(slot)

        @pl.when(jnp.logical_not(inside[di]))
        def _():
            for dj in (-1, 0, 1):
                slot = 4 + 3 * di + dj
                lists[slot] = jnp.zeros((5, ROWS, 128), jnp.int32)
                bounds[slot : slot + 1, :] = jnp.zeros((1, 128), jnp.int32)

    every = [bounds[slot : slot + 1, :] for slot in range(9)]
    number = [jnp.maximum(pltpu.roll(row, 128 - BLOCKS, 1) - row, 0) for row in every]
    over = [
        number[OWN] - OWN_CHUNKS,
        number[1] + number[7] - END_CHUNKS,
        number[0] + number[3] + number[6] - SIDE_CHUNKS,
        number[2] + number[5] + number[8] - SIDE_CHUNKS,
    ]
    most = jnp.maximum(jnp.maximum(over[0], over[1]), jnp.maximum(over[2], over[3]))
    most = jnp.max(jnp.where(lane16[0:1, :] < BLOCKS, most, 0), axis=1, keepdims=True)
    bounds[9:16, :] = jnp.broadcast_to(most, (7, 128))
    to_scalars = pltpu.make_async_copy(bounds, list_bounds, bound_sem.at[1])
    to_scalars.start()
    to_scalars.wait()

    def side_block(b):
        parts = {
            dj: product(lists, dj, b, *chunk_counts(list_bounds, dj, b), 0, SIDE_CHUNKS)
            for dj in (-1, 1)
        }
        k = stress(scales, b)
        raw = [
            jnp.concatenate(
                [
                    own[b, :, c * TZ + half * HALF : c * TZ + (half + 1) * HALF]
                    + parts[dj][:, c * HALF : (c + 1) * HALF]
                    for half, dj in ((0, -1), (1, 1))
                ],
                axis=1,
            )
            for c in range(3)
        ]
        for c, value in enumerate(transformed(k, raw)):
            own[b, :, c * TZ : (c + 1) * TZ] = value

    for b in (0, BLOCKS - 1):
        ranges = chunk_counts(list_bounds, 0, b)
        own[b] += product(lists, 0, jnp.int32(b), *ranges, 0, END_CHUNKS)
    pl.loop(0, BLOCKS, unroll=UNROLL_SIDE)(side_block)
    end_phase(2, counting, total)
    fetch.wait()


def fill_scales(scales, diag, shear):
    scales[0:3, :] = diag[...] * (1.5 / (HALF * HALF))
    scales[3:6, :] = shear[...] * (1.5 / (HALF * HALF))
    scales[6:8, :] = jnp.zeros((2, TY), jnp.float32)


def stress(scales, b):
    return scales[:, pl.ds(pl.multiple_of(b * BLOCK, BLOCK), BLOCK)].T


def transformed(k, raw):
    return (
        k[:, 0:1] * raw[0],
        k[:, 3:4] * raw[0] + k[:, 1:2] * raw[1],
        k[:, 4:5] * raw[0] + k[:, 5:6] * raw[1] + k[:, 2:3] * raw[2],
    )


def chunk_counts(bounds, dj, b):
    slots = [(di + 1) * 3 + dj + 1 for di in (-1, 0, 1)]
    begins = [bounds[slot, b] for slot in slots]
    numbers = [
        jnp.maximum(bounds[slot, BLOCKS + b] - begin, 0) for slot, begin in zip(slots, begins)
    ]
    if dj == 0:
        begins[1] = numbers[1] = 0
    return begins, numbers


def product(lists, dj, b, begins, numbers, start, chunks):
    bf = jnp.bfloat16
    left, right = [], []
    above = numbers[0]
    beside = above + numbers[1]
    every = beside + numbers[2]
    for part in range(chunks):
        i = start + part
        di = jnp.where(i < above, 0, jnp.where(i < beside, 1, 2))
        base = jnp.where(
            i < above,
            begins[0],
            jnp.where(i < beside, begins[1] - above, begins[2] - beside),
        )
        used = i < every
        slot = jnp.where(used, di * 3 + dj + 1, OWN)
        chunk = pl.ds(jnp.where(used, base + i, 0), 1)
        live = jnp.where(used, 1, 0)
        anchor = 128 + b * BLOCK - TY * (di - 1)
        left.append(tent(lists[slot, 0, chunk, :] - anchor, BLOCK, -128))
        q = lists[slot, 1, chunk, :] - 128 + TZ * dj
        if dj == 0:
            shape = tent(q, TZ, -128)
        else:
            shape = tent(q, HALF, -128 if dj < 0 else 0)
        signed = [
            shape * (lists[slot, 2 + c, chunk, :] * live).astype(jnp.float32).astype(bf)
            for c in range(3)
        ]
        right.append(jnp.concatenate(signed, axis=0))
    return lax.dot_general(
        jnp.concatenate(left, axis=1),
        jnp.concatenate(right, axis=1),
        (((1,), (1,)), ((), ())),
        preferred_element_type=jnp.float32,
    )


def tent(place, rows, first):
    bf = jnp.bfloat16
    y = (lax.broadcasted_iota(jnp.int32, (rows, 128), 0) + first).astype(jnp.float32).astype(bf)
    near = jnp.minimum(jnp.maximum(place, -256), 256).astype(jnp.float32).astype(bf)
    return jnp.maximum(bf(HALF) - jnp.abs(y - near), bf(0))


def evaluate(bounds, total, lists, diag, shear, own, mean, out, buffer, acc, scales, out_sem):
    def save(b):
        rows = pl.ds(pl.multiple_of(b * BLOCK, BLOCK), BLOCK)
        return pltpu.make_async_copy(buffer.at[:, rows, :], out.at[:, rows, :], out_sem.at[b])

    gain = jnp.sqrt(TY * GY * (TZ * GZ) / (HALF * HALF) / total[0:1, 0:1])

    def finish(b, field):
        rows = pl.ds(pl.multiple_of(b * BLOCK, BLOCK), BLOCK)
        for c in range(3):
            buffer[c, rows, :] = mean[c, rows, :] + gain * field[:, c * TZ : (c + 1) * TZ]
        save(b).start()

    def leftovers(b):
        begin = bounds[OWN, b]
        number = jnp.maximum(bounds[OWN, BLOCKS + b] - begin, 0)
        jobs = [(0, [0, begin, 0], [0, number, 0], OWN_CHUNKS)]
        for dj, done in ((-1, SIDE_CHUNKS), (0, END_CHUNKS), (1, SIDE_CHUNKS)):
            jobs.append((dj, *chunk_counts(bounds, dj, b), done))
        return jobs

    leftover = bounds[9, 0]

    @pl.when(leftover == 0)
    def _():
        for b in range(BLOCKS):
            finish(b, own.at[b])

    @pl.when(leftover > 0)
    def _():
        @pl.loop(0, BLOCKS)
        def _(b):
            jobs = leftovers(b)
            counts = [numbers[0] + numbers[1] + numbers[2] for _, _, numbers, _ in jobs]
            some = counts[0] > jobs[0][3]
            for count, job in zip(counts[1:], jobs[1:]):
                some = jnp.logical_or(some, count > job[3])

            @pl.when(some)
            def _():
                acc[...] = jnp.zeros_like(acc)
                for count, (dj, begins, numbers, done) in zip(counts, jobs):

                    def more(step, carry, dj=dj, begins=begins, numbers=numbers, done=done):
                        extra = product(lists, dj, b, begins, numbers, done + step * 2, 2)
                        if dj == 0:
                            acc[...] += extra
                        else:
                            for c in range(3):
                                at = c * TZ + (0 if dj < 0 else HALF)
                                acc[:, at : at + HALF] += extra[:, c * HALF : (c + 1) * HALF]
                        return carry

                    lax.fori_loop(0, jnp.maximum(count - done + 1, 0) // 2, more, 0)
                fill_scales(scales, diag, shear)
                raw = [acc[:, c * TZ : (c + 1) * TZ] for c in range(3)]
                for c, value in enumerate(transformed(stress(scales, b), raw)):
                    acc[:, c * TZ : (c + 1) * TZ] = own[b, :, c * TZ : (c + 1) * TZ] + value
                finish(b, acc)

            @pl.when(jnp.logical_not(some))
            def _():
                finish(b, own.at[b])

    for b in range(BLOCKS):
        save(b).wait()


def body(eddy_cells, eddy_signs, eddy_counts, stress_diag, stress_shear, mean_flow):
    vmem = pl.BlockSpec(memory_space=pltpu.VMEM)
    smem = pl.BlockSpec(memory_space=pltpu.SMEM)
    anywhere = pl.BlockSpec(memory_space=pl.ANY)
    hbm = pl.BlockSpec(memory_space=pltpu.HBM)
    dma = pltpu.SemaphoreType.DMA
    f32, i32 = jnp.float32, jnp.int32
    lists, bounds, total, own, held = pl.pallas_call(
        exchange,
        out_shape=(
            pltpu.VMEM((9, 5, ROWS, 128), i32),
            jax.ShapeDtypeStruct((16, 128), jnp.int32),
            pltpu.VMEM((8, 128), f32),
            pltpu.VMEM((BLOCKS, BLOCK, 3 * TZ), f32),
            pltpu.VMEM((3, TY, TZ), f32),
        ),
        in_specs=[hbm, hbm, smem, hbm, hbm, hbm],
        out_specs=(vmem, vmem, vmem, vmem, vmem),
        scratch_shapes=[
            pltpu.VMEM((2, ROWS, 128), jnp.int32),
            pltpu.VMEM((3, 5, ROWS, 128), i32),
            pltpu.VMEM((8, 128), i32),
            pltpu.SMEM((8, 128), i32),
            pltpu.SMEM((16, 128), i32),
            dma((2,)),
            pltpu.VMEM((9, 5, ROWS, 128), i32),
            pltpu.VMEM((8, 128), f32),
            pltpu.VMEM((3, 8, 128), f32),
            pltpu.VMEM((8, 128), f32),
            pltpu.VMEM((3, 8, 128), f32),
            dma((9,)),
            dma((9,)),
            dma((3,)),
            dma((3,)),
            dma((3,)),
            dma((3,)),
            pltpu.VMEM((8, 128), f32),
            pltpu.VMEM((GZ - 1, 8, 128), f32),
            dma((GZ - 1,)),
            dma((GZ - 1,)),
            dma,
            pltpu.VMEM((2, CAP), jnp.int32),
            pltpu.VMEM((3, ROWS, 128), jnp.int32),
            dma((4,)),
            pltpu.VMEM((8, TY), f32),
            pltpu.VMEM((3, TY), f32),
            pltpu.VMEM((3, TY), f32),
        ],
        compiler_params=pltpu.CompilerParams(
            collective_id=0, has_side_effects=True, vmem_limit_bytes=VMEM_LIMIT
        ),
        name="exchange",
    )(
        pltpu.with_memory_space_constraint(eddy_cells.reshape(2, CAP), pltpu.HBM),
        pltpu.with_memory_space_constraint(eddy_signs.reshape(3, ROWS, 128), pltpu.HBM),
        eddy_counts,
        pltpu.with_memory_space_constraint(stress_diag, pltpu.HBM),
        pltpu.with_memory_space_constraint(stress_shear, pltpu.HBM),
        mean_flow,
    )
    return pl.pallas_call(
        evaluate,
        out_shape=jax.ShapeDtypeStruct((3, TY, TZ), f32),
        in_specs=[smem, vmem, vmem, vmem, vmem, vmem, vmem],
        out_specs=anywhere,
        scratch_shapes=[
            pltpu.VMEM((3, TY, TZ), f32),
            pltpu.VMEM((BLOCK, 3 * TZ), f32),
            pltpu.VMEM((8, TY), f32),
            dma((BLOCKS,)),
        ],
        compiler_params=pltpu.CompilerParams(vmem_limit_bytes=VMEM_LIMIT),
        name="evaluate",
    )(bounds, total, lists, stress_diag, stress_shear, own, held)


def solution(mesh):
    return jax.shard_map(
        body,
        mesh=mesh,
        in_specs=(
            P("gy", "gz", None, None),
            P("gy", "gz", None, None),
            P("gy", "gz"),
            P(None, "gy"),
            P(None, "gy"),
            P(None, "gy", "gz"),
        ),
        out_specs=P(None, "gy", "gz"),
        check_vma=False,
    )
```
